32 devices in a mesh: slab: 8 (over z, y), row: 2 (over core), col: 2 (over x).
Axes of the slice: x: 2, y: 2, z: 4, core: 2. Of those that a mesh axis runs over, the one named last changes fastest.
Arguments:
- pressure: float32 [32, 256, 256], P('slab', 'row', 'col'), may hold values from -6 to 6
- velocity: float32 [3, 32, 256, 256], P(None, 'slab', 'row', 'col'), may hold values from -6 to 6
- kappa: float32 [32, 256, 256], P('slab', 'row', 'col'), may hold values from 0.5 to 2
- drive: float32 [32, 256, 256], P('slab', 'row', 'col'), may hold values from -6 to 6
- adj_pressure_in: float32 [32, 256, 256], P('slab', 'row', 'col'), may hold values from -6 to 6
- adj_velocity_in: float32 [3, 32, 256, 256], P(None, 'slab', 'row', 'col'), may hold values from -6 to 6
- wall_mask: int32 [32, 256, 256], P('slab', 'row', 'col'), may hold values 0 or 1
- wall_cells: int32 [8, 2, 2, 512], P('slab', 'row', 'col'), may hold values from 0 to 65535
- wall_rows: int32 [8, 2, 2, 512], P('slab', 'row', 'col'), may hold values from 0 to 2047
- slot_angle: float32 [8, 2, 2, 512], P('slab', 'row', 'col'), may hold values from 0 to 64
- wall_count: int32 [8, 2, 2], P('slab', 'row', 'col'), may hold values from 1 to 512, as said below
- step: int32 [1], replicated, may hold values from 0 to 4095
Outputs:
- adj_pressure: float32 [32, 256, 256], P('slab', 'row', 'col')
- adj_velocity: float32 [3, 32, 256, 256], P(None, 'slab', 'row', 'col')
- shape_grad: float32 [2048, 64], P(('slab', 'row', 'col'))
The draws below stay inside these ranges and needn't reach their ends.
Inputs may be any that keep to these rules, and one draw needn't show every extreme that they name: `wall_count`: some device has all 512 slots live in every draw.
All inputs are finite; a program needn't handle non-finite values. No bound on the sum of `wall_mask` on one device may be relied on, other than what follows from the above.
Results may differ from the reference program's by a relative error of at most 0.00002.
Values sent between devices are 32-bit elements; how exact they have to be, the bound alone decides.
No kernel may reach another device: no remote copies, remote signals or barrier semaphores. Data moves between devices by JAX's collectives and lax.ppermute only.
A program may use at most 64 MiB of HBM per device.

```python
import math
import jax
import jax.numpy as jnp
from jax import lax

CX = 4
CY = 128
CZ = 128
WALL = 512
NROWS = 2048
ANG = 64
NX = 32
NY = 256
NZ = 256
N_SLAB = 8
N_ROW = 2
N_COL = 2


def draw_wall_count(key, part):
    base = jax.random.randint(jax.random.fold_in(key, 1), (N_SLAB, N_ROW, N_COL), 0, WALL, dtype=jnp.int32)
    slab_ids = jnp.arange(N_SLAB, dtype=jnp.int32)[:, None, None] + 1
    counts = 1 + base * slab_ids // N_SLAB
    picked = jax.random.randint(jax.random.fold_in(key, 2), (), 0, N_SLAB * N_ROW * N_COL, dtype=jnp.int32)
    flat = counts.reshape(-1)
    flat = jnp.where(jnp.arange(flat.shape[0], dtype=jnp.int32) == picked, WALL, flat)
    return flat.reshape((N_SLAB, N_ROW, N_COL))


def set_ends(array, key, smallest, top_value):
    longest = array.shape.index(max(array.shape))
    spots = []
    for shift in (0, 1):
        where = [jax.random.randint(jax.random.fold_in(key, axis), (), 0, length) for axis, length in enumerate(array.shape)]
        where[longest] = (where[longest] + shift) % array.shape[longest]
        spots.append(tuple(where))
    return array.at[spots[0]].set(smallest).at[spots[1]].set(top_value)


def level_of(own_key, dims, cuts, smallest, high):
    def one(axis_at, blocks):
        steps = jax.random.uniform(jax.random.fold_in(jax.random.fold_in(own_key, 6), axis_at), (blocks,), jnp.float32, smallest / len(cuts), high / len(cuts))
        return jnp.repeat(jnp.exp(steps), dims[axis_at] // blocks).reshape((-1,) + (1,) * (len(dims) - axis_at - 1))

    factor_of = one(*cuts[0])
    for cut in cuts[1:]:
        factor_of = factor_of * one(*cut)
    return factor_of


def noise(rng, extent, scale, most, cuts=(), held_as=jnp.bfloat16):
    drawn = jax.random.normal(rng, extent, jnp.float32) * scale
    if len(cuts) > 0:
        drawn = level_of(rng, extent, cuts, -0.22, 0.18) * drawn
    return jnp.clip(drawn, min=-most, max=most).astype(held_as)


def setup_inputs(seed: int = 0) -> dict:
    key_list = jax.random.split(jax.random.key(seed), 13)
    pressure = noise(key_list[0], (NX, NY, NZ), 1.0, 6.0, ((0, 8), (1, 2), (2, 2)), jnp.float32)
    velocity = noise(key_list[1], (3, NX, NY, NZ), 1.0, 6.0, ((1, 8), (2, 2), (3, 2)), jnp.float32)
    kappa = jnp.clip(jnp.exp(math.log(2.0) - 1.3862944 * jax.random.uniform(key_list[2], (NX, NY, NZ), jnp.float32) ** level_of(key_list[2], (NX, NY, NZ), ((0, 8), (1, 2), (2, 2)), -0.2, 0.2)), 0.5, 2.0)
    drive = noise(key_list[3], (NX, NY, NZ), 1.0, 6.0, ((0, 8), (1, 2), (2, 2)), jnp.float32)
    adj_pressure_in = noise(key_list[4], (NX, NY, NZ), 1.0, 6.0, ((0, 8), (1, 2), (2, 2)), jnp.float32)
    adj_velocity_in = noise(key_list[5], (3, NX, NY, NZ), 1.0, 6.0, ((1, 8), (2, 2), (3, 2)), jnp.float32)
    wall_mask = set_ends((jax.random.randint(key_list[6], (NX, NY, NZ), 0, 8) < 1).astype(jnp.int32), jax.random.fold_in(key_list[6], 1), 0, 1)
    wall_cells = set_ends(jax.random.randint(key_list[7], (N_SLAB, N_ROW, N_COL, WALL), 0, CX * CY * CZ), jax.random.fold_in(key_list[7], 1), 0, (CX * CY * CZ) - 1).astype(jnp.int32)
    wall_rows = set_ends(jax.random.randint(key_list[8], (N_SLAB, N_ROW, N_COL, WALL), 0, NROWS), jax.random.fold_in(key_list[8], 1), 0, NROWS - 1).astype(jnp.int32)
    slot_angle = jnp.clip(64.0 * jax.random.uniform(key_list[9], (N_SLAB, N_ROW, N_COL, WALL), jnp.float32) ** level_of(key_list[9], (N_SLAB, N_ROW, N_COL, WALL), ((0, 8), (1, 2), (2, 2)), -0.2, 0.2), 0.0, 64.0)
    wall_count = draw_wall_count(jax.random.fold_in(key_list[12], 71), 0)
    step = jax.random.randint(key_list[11], (1,), 0, 4096).astype(jnp.int32)
    return {"pressure": pressure, "velocity": velocity, "kappa": kappa, "drive": drive, "adj_pressure_in": adj_pressure_in, "adj_velocity_in": adj_velocity_in, "wall_mask": wall_mask, "wall_cells": wall_cells, "wall_rows": wall_rows, "slot_angle": slot_angle, "wall_count": wall_count, "step": step}


def centered(field, axis):
    widths = [(0, 0), (0, 0), (0, 0)]
    widths[axis] = (1, 1)
    padded = jnp.pad(field, widths)
    size = padded.shape[axis]
    upper = lax.slice_in_dim(padded, 2, size, axis=axis)
    lower = lax.slice_in_dim(padded, 0, size - 2, axis=axis)
    return (upper - lower) * 0.5


def spline_weights(angle):
    knots = jnp.arange(ANG, dtype=jnp.float32)
    dist = jnp.abs(angle[..., None] - knots)
    dist = jnp.minimum(dist, ANG - dist)
    outer = jnp.maximum(2.0 - dist, 0.0)
    inner = jnp.maximum(1.0 - dist, 0.0)
    return (outer * outer * outer - 4.0 * inner * inner * inner) / 6.0


def reference(pressure, velocity, kappa, drive, adj_pressure_in, adj_velocity_in, wall_mask, wall_cells, wall_rows, slot_angle, wall_count, step):
    open_cells = 1.0 - wall_mask.astype(jnp.float32)
    phase = jnp.cos(0.5 * (step[0] % 97).astype(jnp.float32))
    moved = []
    for comp in range(3):
        value = velocity[comp] - 0.3 * centered(pressure, comp)
        if comp == 0:
            value = value + drive * phase
        moved.append(value)
    scaled = kappa * adj_pressure_in
    total = [adj_velocity_in[comp] + centered(scaled, comp) for comp in range(3)]
    lam_u = [open_cells * total[comp] for comp in range(3)]
    divergence = centered(lam_u[0], 0) + centered(lam_u[1], 1) + centered(lam_u[2], 2)
    adj_pressure = adj_pressure_in + 0.3 * divergence
    sens = -(total[0] * moved[0] + total[1] * moved[1] + total[2] * moved[2])
    slab_ids = jnp.arange(N_SLAB, dtype=jnp.int32)[:, None, None, None]
    row_ids = jnp.arange(N_ROW, dtype=jnp.int32)[None, :, None, None]
    col_ids = jnp.arange(N_COL, dtype=jnp.int32)[None, None, :, None]
    glob_x = slab_ids * CX + wall_cells // (CY * CZ)
    glob_y = row_ids * CY + (wall_cells // CZ) % CY
    glob_z = col_ids * CZ + wall_cells % CZ
    values = sens[glob_x, glob_y, glob_z]
    live = jnp.arange(WALL, dtype=jnp.int32) < wall_count[..., None]
    values = jnp.where(live, values, 0.0)
    contrib = values[..., None] * spline_weights(slot_angle)
    shape_grad = jnp.zeros((NROWS, ANG), jnp.float32).at[wall_rows.reshape(-1)].add(contrib.reshape(-1, ANG))
    return adj_pressure, jnp.stack(lam_u), shape_grad
```

```python
import jax
import jax.numpy as jnp
from jax import lax
from jax.experimental import pallas as pl
from jax.experimental.pallas import tpu as pltpu
from jax.sharding import PartitionSpec as P

NROWS = 2048
ANG = 64
F32 = jnp.float32
BF16 = jnp.bfloat16
VM = pl.BlockSpec(memory_space=pltpu.VMEM)
SM = pl.BlockSpec(memory_space=pltpu.SMEM)
LIMIT = pltpu.CompilerParams(vmem_limit_bytes=24 << 20)


def call(body, outs, args, specs, scratch=(), flops=1_000_000, moved=1_000_000):
    return pl.pallas_call(
        body,
        out_shape=outs,
        in_specs=specs,
        out_specs=jax.tree.map(lambda _: VM, outs),
        scratch_shapes=list(scratch),
        compiler_params=LIMIT,
        cost_estimate=pl.CostEstimate(flops=flops, bytes_accessed=moved, transcendentals=0),
    )(*args)


def shape(dims, dtype=F32):
    return jax.ShapeDtypeStruct(tuple(dims), dtype)


def is_odd(axis):
    return lax.rem(lax.axis_index(axis), 2) == 1


def swap_pairs(count, first):
    pairs = []
    for low in range(first, count - 1, 2):
        pairs += [(low, low + 1), (low + 1, low)]
    return pairs


def swap(axis, first, message):
    return lax.ppermute(message, axis, swap_pairs(lax.axis_size(axis), first))


def slab_faces(p_ref, k_ref, a_ref, *out_refs):
    last = p_ref.shape[0] - 1
    odd = is_odd("slab")
    for first, out_ref in enumerate(out_refs):
        at = jnp.where(odd != (first == 1), 0, last)
        out_ref[0] = p_ref[at]
        out_ref[1] = k_ref[at] * a_ref[at]


def side_faces(rounds, p_ref, k_ref, a_ref, t_ref, m_ref, *out_refs):
    depth, height, width = p_ref.shape
    lanes = lax.broadcasted_iota(jnp.int32, (height, width), 1)
    for (axis, first), out_ref in zip(rounds, out_refs):
        high = is_odd(axis) == (first == 1)
        sign = jnp.where(high, -0.5, 0.5)
        if axis == "row":
            at = jnp.where(high, height - 1, 0)
            inner = jnp.where(high, height - 2, 1)
            for x in range(depth):
                face, second = pl.ds(at, 1), pl.ds(inner, 1)
                free = 1.0 - m_ref[x, face, :].astype(F32)
                out_ref[0, pl.ds(x, 1), :] = p_ref[x, face, :]
                out_ref[1, pl.ds(x, 1), :] = k_ref[x, face, :] * a_ref[x, face, :]
                behind = k_ref[x, second, :] * a_ref[x, second, :]
                out_ref[2, pl.ds(x, 1), :] = free * (t_ref[1, x, face, :] + sign * behind)
                out_ref[3, pl.ds(x, 1), :] = free
        else:
            at = jnp.where(high, width - 1, 0)
            turn = jnp.where(high, 1, width - 1)
            table = jnp.zeros((height, width), F32)
            for x in range(depth):
                free = 1.0 - m_ref[x].astype(F32)
                scaled = k_ref[x] * a_ref[x]
                behind = pltpu.roll(scaled, turn, 1)
                fields = (p_ref[x], scaled, free * (t_ref[2, x] + sign * behind), free)
                for f, field in enumerate(fields):
                    lane = f * depth + x
                    moved = pltpu.roll(field, lax.rem(lane - at + width, width), 1)
                    table = jnp.where(lanes == lane, moved, table)
            flipped = table.T
            for f in range(4):
                out_ref[f] = flipped[f * depth : (f + 1) * depth]


def low_high(axis, first, second):
    odd = is_odd(axis)
    zero = jnp.zeros_like(first)
    second = zero if second is None else second
    return jnp.where(odd, first, second), jnp.where(odd, second, first)


def side(field, axis, low, high):
    size = field.shape[axis]
    at = lax.broadcasted_iota(jnp.int32, field.shape, axis)
    upper = jnp.where(at == size - 1, high, pltpu.roll(field, size - 1, axis))
    lower = jnp.where(at == 0, low, pltpu.roll(field, 1, axis))
    return (upper - lower) * 0.5


def halves(value):
    top = value.astype(BF16)
    rest = value - top.astype(F32)
    mid = rest.astype(BF16)
    return top, mid, (rest - mid.astype(F32)).astype(BF16)


def take_halo(axis, refs):
    first = refs[0][...]
    second = refs[1][...] if len(refs) > 1 else None
    return low_high(axis, first, second)


def columns(halo, height, width):
    depth = halo.shape[1]
    table = jnp.concatenate([halo[f] for f in range(halo.shape[0])], axis=0)
    table = jnp.concatenate([table, jnp.zeros((width - table.shape[0], height), F32)], axis=0)
    return table.T


def main_body(n_slab, n_row, n_col, refs):
    p_ref, v_ref, k_ref, d_ref, a_ref, t_ref, m_ref, c_ref, r_ref, g_ref, n_ref, ph_ref = refs[:12]
    rest = refs[12:]
    slab_refs, rest = rest[:n_slab], rest[n_slab:]
    row_refs, rest = rest[:n_row], rest[n_row:]
    col_refs, rest = rest[:n_col], rest[n_col:]
    lam_ref, slot_ref = rest[:2]
    face_refs = rest[2 : 2 + n_slab]
    q_ref, sens_ref = rest[2 + n_slab :]
    depth, height, width = p_ref.shape
    phase = ph_ref[0]
    slab_low, slab_high = take_halo("slab", slab_refs)
    row_low, row_high = take_halo("row", row_refs)
    col_low, col_high = (columns(h, height, width) for h in take_halo("col", col_refs))
    for x in range(depth):
        q_ref[x] = k_ref[x] * a_ref[x]
    for x in range(depth):
        p, q = p_ref[x], q_ref[x]

        def along(field, ref, which):
            upper = ref[x + 1] if x + 1 < depth else slab_high[which]
            lower = ref[x - 1] if x > 0 else slab_low[which]
            lane = which * depth + x
            return (
                (upper - lower) * 0.5,
                side(field, 0, row_low[which, x : x + 1], row_high[which, x : x + 1]),
                side(field, 1, col_low[:, lane : lane + 1], col_high[:, lane : lane + 1]),
            )

        slopes = along(p, p_ref, 0)
        gains = along(q, q_ref, 1)
        free = 1.0 - m_ref[x].astype(F32)
        sens = jnp.zeros((height, width), F32)
        for comp in range(3):
            total = t_ref[comp, x] + gains[comp]
            lam_ref[comp, x] = free * total
            moved = v_ref[comp, x] - 0.3 * slopes[comp]
            if comp == 0:
                moved = moved + d_ref[x] * phase
            sens = sens + total * moved
        sens_ref[pl.ds(x * height, height), :] = -sens
    odd = is_odd("slab")
    for first, face_ref in enumerate(face_refs):
        face_ref[...] = lam_ref[0, jnp.where(odd != (first == 1), 0, depth - 1)]
    cells = c_ref[...]
    slots = cells.shape[1]
    lines = depth * height
    line = lax.div(cells, width)
    picks = lax.broadcasted_iota(jnp.int32, (lines, slots), 0) == line
    picks = jnp.where(picks, 1.0, 0.0).astype(BF16)
    found = jnp.zeros((width, slots), F32)
    for piece in halves(sens_ref[...]):
        found = found + lax.dot_general(
            piece, picks, (((0,), (0,)), ((), ())), preferred_element_type=F32
        )
    lane = lax.broadcasted_iota(jnp.int32, (width, slots), 0)
    values = jnp.sum(jnp.where(lane == cells - line * width, found, 0.0), axis=0, keepdims=True)
    live = lax.broadcasted_iota(jnp.int32, (1, slots), 1) < n_ref[0]
    values = jnp.where(live, values, 0.0)
    rows = r_ref[...].astype(F32)
    angles = g_ref[...]
    for j in range(slots // 128):
        part = slice(128 * j, 128 * (j + 1))
        slot_ref[0, pl.ds(j, 1), :] = values[:, part]
        slot_ref[1, pl.ds(j, 1), :] = rows[:, part]
        slot_ref[2, pl.ds(j, 1), :] = angles[:, part]


def pressure_body(n_slab, n_row, n_col, refs):
    lam_ref, k_ref, a_ref = refs[:3]
    rest = refs[3:]
    face_refs, rest = rest[:n_slab], rest[n_slab:]
    row_refs, rest = rest[:n_row], rest[n_row:]
    col_refs, (out_ref,) = rest[:n_col], rest[n_col:]
    depth, height, width = a_ref.shape
    slab_low, slab_high = take_halo("slab", face_refs)
    row_low, row_high = take_halo("row", row_refs)
    col_low, col_high = (columns(h, height, width) for h in take_halo("col", col_refs))
    for x in range(depth):
        scaled = k_ref[x] * a_ref[x]
        half = 0.5 * scaled
        one = slice(x, x + 1)
        push, open_at = slice(2 * depth + x, 2 * depth + x + 1), slice(3 * depth + x, 3 * depth + x + 1)
        upper = lam_ref[0, x + 1] if x + 1 < depth else slab_high
        lower = lam_ref[0, x - 1] if x > 0 else slab_low
        row_above = row_high[2, one] - row_high[3, one] * half[height - 1 :]
        row_below = row_low[2, one] + row_low[3, one] * half[:1]
        col_above = col_high[:, push] - col_high[:, open_at] * half[:, width - 1 :]
        col_below = col_low[:, push] + col_low[:, open_at] * half[:, :1]
        spread = (
            (upper - lower) * 0.5
            + side(lam_ref[1, x], 0, row_below, row_above)
            + side(lam_ref[2, x], 1, col_below, col_above)
        )
        out_ref[x] = a_ref[x] + 0.3 * spread


def dense_body(block, n_slots, n_prior, refs):
    slot_refs = refs[:n_slots]
    prior = refs[n_slots : n_slots + n_prior]
    out_ref, pick_ref, *piece_refs = refs[n_slots + n_prior :]
    base = (lax.axis_index("slab") * block).astype(F32)
    here = lax.broadcasted_iota(jnp.int32, (block, 128), 0).astype(F32) + base
    knots = lax.broadcasted_iota(jnp.int32, (ANG, 128), 0).astype(F32)
    at = 0
    for slot_ref in slot_refs:
        for d in range(slot_ref.shape[0] // 3):
            for j in range(slot_ref.shape[1]):
                value = slot_ref[3 * d, pl.ds(j, 1), :]
                row = slot_ref[3 * d + 1, pl.ds(j, 1), :]
                angle = slot_ref[3 * d + 2, pl.ds(j, 1), :]
                lanes = pl.ds(at, 128)
                pick_ref[:, lanes] = jnp.where(here == row, 1.0, 0.0).astype(BF16)
                dist = jnp.abs(angle - knots)
                dist = jnp.minimum(dist, ANG - dist)
                outer = jnp.maximum(2.0 - dist, 0.0)
                inner = jnp.maximum(1.0 - dist, 0.0)
                weight = (outer * outer * outer - 4.0 * inner * inner * inner) * (1.0 / 6.0)
                for piece, piece_ref in zip(halves(value * weight), piece_refs):
                    piece_ref[:, lanes] = piece
                at += 128
    total = prior[0][...] if prior else jnp.zeros(out_ref.shape, F32)
    for piece_ref in piece_refs:
        total = total + lax.dot_general(
            pick_ref[...], piece_ref[...], (((1,), (1,)), ((), ())), preferred_element_type=F32
        )
    out_ref[...] = total


def dense(block, slots, prior=()):
    count = sum(s.shape[0] // 3 * s.shape[1] * 128 for s in slots)

    def body(*refs):
        dense_body(block, len(slots), len(prior), refs)

    return call(
        body,
        shape((block, ANG)),
        (*slots, *prior),
        [VM] * (len(slots) + len(prior)),
        [pltpu.VMEM((block, count), BF16)] + [pltpu.VMEM((ANG, count), BF16)] * 3,
    )


def share_and_add(slots, axis, block):
    count = lax.axis_size(axis)
    have = slots
    step = 1
    total = None
    while step < count:
        got = lax.ppermute(have, axis, [(i, i ^ step) for i in range(count)])
        if 2 * step < count:
            have = jnp.concatenate([have, got], axis=0)
        else:
            total = dense(block, (have,))
            total = dense(block, (got,), (total,))
        step *= 2
    return dense(block, (have,)) if total is None else total


def halve(total, axis):
    count = lax.axis_size(axis)
    me = lax.axis_index(axis)
    step = count // 2
    while step > 0:
        half = total.shape[0] // 2
        bit = lax.rem(me // step, 2)
        sent = lax.dynamic_slice_in_dim(total, (1 - bit) * half, half, axis=0)
        kept = lax.dynamic_slice_in_dim(total, bit * half, half, axis=0)
        total = kept + lax.ppermute(sent, axis, [(i, i ^ step) for i in range(count)])
        step //= 2
    return total


def rounds_of(axis):
    return [(axis, first) for first in (0, 1) if swap_pairs(lax.axis_size(axis), first)]


def local(
    pressure,
    velocity,
    kappa,
    drive,
    adj_pressure_in,
    adj_velocity_in,
    wall_mask,
    wall_cells,
    wall_rows,
    slot_angle,
    wall_count,
    step,
):
    depth, height, width = pressure.shape
    slots = wall_cells.size
    phase = jnp.cos(0.5 * (step % 97).astype(F32))
    slab_rounds, row_rounds, col_rounds = (rounds_of(a) for a in ("slab", "row", "col"))
    faces = call(
        slab_faces,
        [shape((2, height, width))] * len(slab_rounds),
        (pressure, kappa, adj_pressure_in),
        [VM] * 3,
    )
    slab_got = [swap(axis, first, m) for (axis, first), m in zip(slab_rounds, faces)]
    side_rounds = row_rounds + col_rounds
    outs = [shape((4, depth, width if axis == "row" else height)) for axis, _ in side_rounds]

    def sides(*refs):
        side_faces(side_rounds, *refs)

    messages = call(
        sides,
        outs,
        (pressure, kappa, adj_pressure_in, adj_velocity_in, wall_mask),
        [VM] * 5,
    )
    side_got = [swap(axis, first, m) for (axis, first), m in zip(side_rounds, messages)]
    counts = (len(slab_rounds), len(row_rounds), len(col_rounds))

    def main(*refs):
        main_body(*counts, refs)

    flat = (1, slots)
    lam, mine, *lam_faces = call(
        main,
        [shape((3, depth, height, width)), shape((3, slots // 128, 128))]
        + [shape((height, width))] * len(slab_rounds),
        (
            pressure,
            velocity,
            kappa,
            drive,
            adj_pressure_in,
            adj_velocity_in,
            wall_mask,
            wall_cells.reshape(flat),
            wall_rows.reshape(flat),
            slot_angle.reshape(flat),
            wall_count.reshape(1),
            phase,
            *slab_got,
            *side_got,
        ),
        [VM] * 10 + [SM] * 2 + [VM] * sum(counts),
        [pltpu.VMEM((depth, height, width), F32), pltpu.VMEM((depth * height, width), F32)],
    )
    lam_got = [swap(axis, first, m) for (axis, first), m in zip(slab_rounds, lam_faces)]

    def pressure_step(*refs):
        pressure_body(*counts, refs)

    adj_pressure = call(
        pressure_step,
        shape((depth, height, width)),
        (lam, kappa, adj_pressure_in, *lam_got, *side_got),
        [VM] * (3 + sum(counts)),
    )
    total = share_and_add(mine, "slab", NROWS // lax.axis_size("slab"))
    total = halve(halve(total, "row"), "col")
    return (adj_pressure, lam, total)


def solution(mesh):
    in_specs = (
        P("slab", "row", "col"),
        P(None, "slab", "row", "col"),
        P("slab", "row", "col"),
        P("slab", "row", "col"),
        P("slab", "row", "col"),
        P(None, "slab", "row", "col"),
        P("slab", "row", "col"),
        P("slab", "row", "col", None),
        P("slab", "row", "col", None),
        P("slab", "row", "col", None),
        P("slab", "row", "col"),
        P(),
    )
    out_specs = (
        P("slab", "row", "col"),
        P(None, "slab", "row", "col"),
        P(("slab", "row", "col"), None),
    )
    return jax.shard_map(local, mesh=mesh, in_specs=in_specs, out_specs=out_specs, check_vma=False)
```

```python
import jax
import jax.numpy as jnp
from jax import lax
from jax.experimental import pallas as pl
from jax.experimental.pallas import tpu as pltpu
from jax.sharding import PartitionSpec as P


NROWS = 2048
ANG = 64
F32 = jnp.float32
BF16 = jnp.bfloat16
VM = pl.BlockSpec(memory_space=pltpu.VMEM)
HB = pl.BlockSpec(memory_space=pltpu.HBM)
SM = pl.BlockSpec(memory_space=pltpu.SMEM)
LIMIT = pltpu.CompilerParams(vmem_limit_bytes=24 << 20)


def call(body, outs, args, specs, scratch=(), out_specs=None):
    return pl.pallas_call(
        body,
        out_shape=outs,
        in_specs=specs,
        out_specs=jax.tree.map(lambda _: VM, outs) if out_specs is None else out_specs,
        scratch_shapes=list(scratch),
        compiler_params=LIMIT,
        cost_estimate=pl.CostEstimate(flops=1_000_000, bytes_accessed=1_000_000, transcendentals=0),
    )(*args)


def fetch(pairs, sems):
    copies = [pltpu.make_async_copy(s, d, sems.at[i]) for i, (s, d) in enumerate(pairs)]
    for copy in copies:
        copy.start()
    return copies


def shape(dims, dtype=F32):
    return jax.ShapeDtypeStruct(tuple(dims), dtype)


def is_odd(axis):
    return lax.rem(lax.axis_index(axis), 2) == 1


def swap_pairs(count, first):
    pairs = []
    for low in range(first, count - 1, 2):
        pairs += [(low, low + 1), (low + 1, low)]
    return pairs


def swap(axis, first, message):
    return lax.ppermute(message, axis, swap_pairs(lax.axis_size(axis), first))


def faces_body(rounds, refs):
    p_ref, k_ref, a_ref = refs[:3]
    outs, (pv_ref, qv_ref, av_ref, kv_ref, sems) = refs[3 : 3 + len(rounds)], refs[3 + len(rounds) :]
    depth = pv_ref.shape[0]
    copies = fetch(((k_ref, kv_ref), (a_ref, av_ref), (p_ref, pv_ref)), sems)
    copies[0].wait()
    copies[1].wait()
    for x in range(depth):
        qv_ref[x] = kv_ref[x] * av_ref[x]
    copies[2].wait()
    odd = is_odd("slab")
    for (_, first), out_ref in zip(rounds, outs):
        at = jnp.where(odd != (first == 1), 0, depth - 1)
        out_ref[0] = pv_ref[at]
        out_ref[1] = qv_ref[at]


def sides_body(rounds, refs):
    pv_ref, qv_ref, t_ref, m_ref = refs[:4]
    outs, (tv_ref, free_ref, mv_ref, sems) = refs[4 : 4 + len(rounds)], refs[4 + len(rounds) :]
    depth, height, width = pv_ref.shape
    copies = fetch(((m_ref, mv_ref), (t_ref, tv_ref)), sems)
    copies[0].wait()
    for x in range(depth):
        free_ref[x] = 1.0 - mv_ref[x].astype(F32)
    copies[1].wait()
    lanes = lax.broadcasted_iota(jnp.int32, (height, width), 1)
    for (axis, first), out_ref in zip(rounds, outs):
        high = is_odd(axis) == (first == 1)
        sign = jnp.where(high, -0.5, 0.5)
        if axis == "row":
            at = jnp.where(high, height - 1, 0)
            inner = jnp.where(high, height - 2, 1)
            for x in range(depth):
                face, second = pl.ds(at, 1), pl.ds(inner, 1)
                free = free_ref[x, face, :]
                out_ref[0, pl.ds(x, 1), :] = pv_ref[x, face, :]
                out_ref[1, pl.ds(x, 1), :] = qv_ref[x, face, :]
                out_ref[2, pl.ds(x, 1), :] = free * (tv_ref[1, x, face, :] + sign * qv_ref[x, second, :])
                out_ref[3, pl.ds(x, 1), :] = free
        else:
            at = jnp.where(high, width - 1, 0)
            turn = jnp.where(high, 1, width - 1)
            table = jnp.zeros((height, width), F32)
            for x in range(depth):
                free, scaled = free_ref[x], qv_ref[x]
                behind = pltpu.roll(scaled, turn, 1)
                fields = (pv_ref[x], scaled, free * (tv_ref[2, x] + sign * behind), free)
                for f, field in enumerate(fields):
                    lane = f * depth + x
                    moved = pltpu.roll(field, lax.rem(lane - at + width, width), 1)
                    table = jnp.where(lanes == lane, moved, table)
            flipped = table.T
            for f in range(4):
                out_ref[f] = flipped[f * depth : (f + 1) * depth]


def take_halo(axis, refs):
    odd = is_odd(axis)
    first = refs[0][...]
    second = refs[1][...] if len(refs) > 1 else jnp.zeros_like(first)
    return jnp.where(odd, first, second), jnp.where(odd, second, first)


def side(field, axis, low, high):
    size = field.shape[axis]
    at = lax.broadcasted_iota(jnp.int32, field.shape, axis)
    upper = jnp.where(at == size - 1, high, pltpu.roll(field, size - 1, axis))
    lower = jnp.where(at == 0, low, pltpu.roll(field, 1, axis))
    return (upper - lower) * 0.5


def halves(value):
    top = value.astype(BF16)
    rest = value - top.astype(F32)
    mid = rest.astype(BF16)
    return top, mid, (rest - mid.astype(F32)).astype(BF16)


def inner_body(pv_ref, qv_ref, tv_ref, v_ref, d_ref, c_ref, r_ref, g_ref, ph_ref,
               total_ref, moved_ref, pick_ref, slot_in_ref, vv_ref, dv_ref, sems):
    depth, _, width = pv_ref.shape
    copies = fetch(
        (
            (c_ref, slot_in_ref.at[0]),
            (v_ref, vv_ref),
            (d_ref, dv_ref),
        ),
        sems,
    )
    for x in range(depth):
        q = qv_ref[x]
        upper = qv_ref[x + 1] if x + 1 < depth else 0.0
        lower = qv_ref[x - 1] if x > 0 else 0.0
        total_ref[0, x] = tv_ref[0, x] + (upper - lower) * 0.5
        total_ref[1, x] = tv_ref[1, x] + side(q, 0, 0.0, 0.0)
        total_ref[2, x] = tv_ref[2, x] + side(q, 1, 0.0, 0.0)
    copies[0].wait()
    cells = slot_in_ref[0]
    line = lax.div(cells, width)
    at = lax.broadcasted_iota(jnp.int32, pick_ref.shape, 0)
    pick_ref[...] = jnp.where(at == line, 1.0, 0.0).astype(BF16)
    copies[1].wait()
    copies[2].wait()
    phase = ph_ref[0]
    for x in range(depth):
        p = pv_ref[x]
        upper = pv_ref[x + 1] if x + 1 < depth else 0.0
        lower = pv_ref[x - 1] if x > 0 else 0.0
        moved_ref[0, x] = vv_ref[0, x] - 0.3 * ((upper - lower) * 0.5) + dv_ref[x] * phase
        moved_ref[1, x] = vv_ref[1, x] - 0.3 * side(p, 0, 0.0, 0.0)
        moved_ref[2, x] = vv_ref[2, x] - 0.3 * side(p, 1, 0.0, 0.0)


def edge_table(low, high, height, width):
    count = low.shape[0]
    lines = []
    for i in range(count):
        lines += [low[i : i + 1], high[i + 1 : i + 2] if i + 1 < count else None]
    lines = [l for l in lines if l is not None]
    fill = jnp.zeros((width - 2 * count, height), F32)
    return jnp.concatenate(lines + [fill, high[:1]], axis=0).T


def main_body(counts, refs):
    total_ref, moved_ref, free_ref, pick_ref, cell_ref, row_ref, angle_ref, n_ref = refs[:8]
    rest = refs[8:]
    n_slab, n_row, n_col = counts
    slab_refs, rest = rest[:n_slab], rest[n_slab:]
    row_refs, rest = rest[:n_row], rest[n_row:]
    col_refs, rest = rest[:n_col], rest[n_col:]
    lam_ref, slot_ref, *face_refs, sens_ref = rest
    _, depth, height, width = total_ref.shape
    slab_low, slab_high = take_halo("slab", slab_refs)
    row_low, row_high = take_halo("row", row_refs)
    col_low, col_high = take_halo("col", col_refs)
    low = jnp.concatenate([col_low[0] * 0.15, col_low[1] * -0.5], axis=0)
    high = jnp.concatenate([col_high[0] * -0.15, col_high[1] * 0.5], axis=0)
    edges = edge_table(low, high, height, width)
    lanes = lax.broadcasted_iota(jnp.int32, (8, width), 1)
    is_edge = (lanes == 0) | (lanes == width - 1)
    tall = lax.broadcasted_iota(jnp.int32, (8, width), 0)
    for x in range(depth):
        for y in range(0, height, 8):
            at = slice(y, y + 8)
            totals = [total_ref[c, x, at] for c in range(3)]
            moves = [moved_ref[c, x, at] for c in range(3)]
            if x == 0:
                totals[0] = totals[0] - 0.5 * slab_low[1, at]
                moves[0] = moves[0] + 0.15 * slab_low[0, at]
            if x == depth - 1:
                totals[0] = totals[0] + 0.5 * slab_high[1, at]
                moves[0] = moves[0] - 0.15 * slab_high[0, at]
            one = slice(x, x + 1)
            if y == 0:
                totals[1] = totals[1] - jnp.where(tall == 0, 0.5 * row_low[1, one], 0.0)
                moves[1] = moves[1] + jnp.where(tall == 0, 0.15 * row_low[0, one], 0.0)
            if y == height - 8:
                totals[1] = totals[1] + jnp.where(tall == 7, 0.5 * row_high[1, one], 0.0)
                moves[1] = moves[1] - jnp.where(tall == 7, 0.15 * row_high[0, one], 0.0)
            for which, terms in ((1, totals), (0, moves)):
                shift = (width - 2 * (which * depth + x)) % width
                turned = pltpu.roll(edges[at], shift, 1) if shift else edges[at]
                terms[2] = terms[2] + jnp.where(is_edge, turned, 0.0)
            free = free_ref[x, at]
            sens = totals[0] * moves[0] + totals[1] * moves[1] + totals[2] * moves[2]
            for c in range(3):
                lam_ref[c, x, at] = free * totals[c]
            sens_ref[pl.ds(x * height + y, 8), :] = -sens
    odd = is_odd("slab")
    for first, face_ref in enumerate(face_refs):
        face_ref[...] = lam_ref[0, jnp.where(odd != (first == 1), 0, depth - 1)]
    cells = cell_ref[...]
    slots = cells.shape[1]
    pieces = jnp.concatenate(halves(sens_ref[...].T), axis=0)
    found = jnp.dot(pieces, pick_ref[...], preferred_element_type=F32)
    found = found[:width] + found[width : 2 * width] + found[2 * width :]
    lane = lax.broadcasted_iota(jnp.int32, (width, slots), 0)
    values = jnp.sum(jnp.where(lane == lax.rem(cells, width), found, 0.0), axis=0, keepdims=True)
    live = lax.broadcasted_iota(jnp.int32, (1, slots), 1) < n_ref[0]
    values = jnp.where(live, values, 0.0)
    rows = row_ref[...].astype(F32)
    angles = angle_ref[...]
    for j in range(slots // 128):
        part = slice(128 * j, 128 * (j + 1))
        slot_ref[0, pl.ds(j, 1), :] = values[:, part]
        slot_ref[1, pl.ds(j, 1), :] = rows[:, part]
        slot_ref[2, pl.ds(j, 1), :] = angles[:, part]


def columns(halo, height, width):
    table = jnp.concatenate([halo[2], halo[3]], axis=0)
    table = jnp.concatenate([table, jnp.zeros((width - table.shape[0], height), F32)], axis=0)
    return table.T


def part_body(counts, refs):
    lam_ref, qv_ref, av_ref = refs[:3]
    rest = refs[3:]
    _, n_row, n_col = counts
    row_refs, rest = rest[:n_row], rest[n_row:]
    col_refs, (part_ref, out_ref, sems) = rest[:n_col], rest[n_col:]
    copies = fetch(((lam_ref, out_ref),), sems)
    depth, height, width = av_ref.shape
    row_low, row_high = take_halo("row", row_refs)
    col_low, col_high = (columns(h, height, width) for h in take_halo("col", col_refs))
    for x in range(depth):
        half = 0.5 * qv_ref[x]
        one = slice(x, x + 1)
        free = slice(depth + x, depth + x + 1)
        upper = lam_ref[0, x + 1] if x + 1 < depth else 0.0
        lower = lam_ref[0, x - 1] if x > 0 else 0.0
        row_above = row_high[2, one] - row_high[3, one] * half[height - 1 :]
        row_below = row_low[2, one] + row_low[3, one] * half[:1]
        col_above = col_high[:, one] - col_high[:, free] * half[:, width - 1 :]
        col_below = col_low[:, one] + col_low[:, free] * half[:, :1]
        spread = (
            (upper - lower) * 0.5
            + side(lam_ref[1, x], 0, row_below, row_above)
            + side(lam_ref[2, x], 1, col_below, col_above)
        )
        part_ref[x] = av_ref[x] + 0.3 * spread
    copies[0].wait()


def fix_body(refs):
    part_ref, *face_refs, out_ref = refs
    depth = part_ref.shape[0]
    low, high = take_halo("slab", face_refs)
    for x in range(depth):
        value = part_ref[x]
        if x == 0:
            value = value - 0.15 * low
        if x == depth - 1:
            value = value + 0.15 * high
        out_ref[x] = value


def dense_body(block, n_slots, n_prior, refs):
    slot_refs = refs[:n_slots]
    prior = refs[n_slots : n_slots + n_prior]
    out_ref, pick_ref, piece_ref = refs[n_slots + n_prior :]
    base = (lax.axis_index("slab") * block).astype(F32)
    here = lax.broadcasted_iota(jnp.int32, (block, 128), 0).astype(F32) + base
    knots = lax.broadcasted_iota(jnp.int32, (ANG, 128), 0).astype(F32)
    at = 0
    for slot_ref in slot_refs:
        for d in range(slot_ref.shape[0] // 3):
            for j in range(slot_ref.shape[1]):
                value = slot_ref[3 * d, pl.ds(j, 1), :] * (1.0 / 6.0)
                row = slot_ref[3 * d + 1, pl.ds(j, 1), :]
                angle = slot_ref[3 * d + 2, pl.ds(j, 1), :]
                lanes = pl.ds(at, 128)
                pick_ref[:, lanes] = jnp.where(here == row, 1.0, 0.0).astype(BF16)
                dist = jnp.abs(angle - knots)
                dist = jnp.minimum(dist, ANG - dist)
                outer = jnp.maximum(2.0 - dist, 0.0)
                inner = jnp.maximum(1.0 - dist, 0.0)
                weight = outer * outer * outer - 4.0 * (inner * inner * inner)
                piece_ref[:, lanes] = jnp.concatenate(halves(value * weight), axis=0)
                at += 128
    total = lax.dot_general(
        piece_ref[...], pick_ref[...], (((1,), (1,)), ((), ())), preferred_element_type=F32
    )
    total = (total[:ANG] + total[ANG : 2 * ANG] + total[2 * ANG :]).T
    out_ref[...] = total + prior[0][...] if prior else total


def dense(block, slots, prior=()):
    count = sum(s.shape[0] // 3 * s.shape[1] * 128 for s in slots)

    def body(*refs):
        dense_body(block, len(slots), len(prior), refs)

    return call(
        body,
        shape((block, ANG)),
        (*slots, *prior),
        [VM] * (len(slots) + len(prior)),
        [pltpu.VMEM((block, count), BF16), pltpu.VMEM((3 * ANG, count), BF16)],
    )


def share_and_add(slots, axis, block):
    count = lax.axis_size(axis)
    have = slots
    total = None
    for k in range(count.bit_length() - 1):
        got = lax.ppermute(have, axis, [(i, i ^ (1 << k)) for i in range(count)])
        if 2 << k < count:
            have = jnp.concatenate([have, got], axis=0)
        else:
            total = dense(block, (have,))
            total = dense(block, (got,), (total,))
    return dense(block, (have,)) if total is None else total


def halve(total, axis):
    count = lax.axis_size(axis)
    me = lax.axis_index(axis)
    step = count // 2
    while step > 0:
        half = total.shape[0] // 2
        bit = lax.rem(me // step, 2)
        sent = lax.dynamic_slice_in_dim(total, (1 - bit) * half, half, axis=0)
        kept = lax.dynamic_slice_in_dim(total, bit * half, half, axis=0)
        total = kept + lax.ppermute(sent, axis, [(i, i ^ step) for i in range(count)])
        step //= 2
    return total


def rounds_of(axis):
    return [(axis, first) for first in (0, 1) if swap_pairs(lax.axis_size(axis), first)]


def swap_all(rounds, messages):
    got = []
    for (axis, first), message in zip(rounds, messages):
        got.append(swap(axis, first, message))
    return got


def step_back(
    pressure,
    velocity,
    kappa,
    drive,
    adj_pressure_in,
    adj_velocity_in,
    wall_mask,
    wall_cells,
    wall_rows,
    slot_angle,
    wall_count,
    step,
):
    grid = depth, height, width = pressure.shape
    slots = wall_cells.size
    flat = (1, slots)
    sems = pltpu.SemaphoreType.DMA
    phase = jnp.cos(0.5 * (step % 97).astype(F32))
    slab_rounds, row_rounds, col_rounds = (rounds_of(a) for a in ("slab", "row", "col"))
    side_rounds = row_rounds + col_rounds
    counts = (len(slab_rounds), len(row_rounds), len(col_rounds))

    *faces, p_in, q_in, a_in = call(
        lambda *refs: faces_body(slab_rounds, refs),
        [shape((2, height, width))] * counts[0] + [shape(grid)] * 3,
        (pressure, kappa, adj_pressure_in),
        [HB] * 3,
        [pltpu.VMEM(grid, F32), sems((3,))],
    )
    slab_got = swap_all(slab_rounds, faces)
    *messages, t_in, free = call(
        lambda *refs: sides_body(side_rounds, refs),
        [shape((4, depth, width if axis == "row" else height)) for axis, _ in side_rounds]
        + [shape((3, *grid)), shape(grid)],
        (p_in, q_in, adj_velocity_in, wall_mask),
        [VM] * 2 + [HB] * 2,
        [pltpu.VMEM(grid, jnp.int32), sems((2,))],
    )
    side_got = swap_all(side_rounds, messages)
    total, moved, picks, cells = call(
        inner_body,
        [
            shape((3, *grid)),
            shape((3, *grid)),
            shape((depth * height, slots), BF16),
            shape((1, 1, slots), jnp.int32),
        ],
        (
            p_in,
            q_in,
            t_in,
            velocity,
            drive,
            wall_cells.reshape(flat),
            wall_rows.reshape(flat),
            slot_angle.reshape(flat),
            phase,
        ),
        [VM] * 3 + [HB] * 5 + [SM],
        [pltpu.VMEM((3, *grid), F32), pltpu.VMEM(grid, F32), sems((3,))],
    )
    lam, mine, *lam_faces = call(
        lambda *refs: main_body(counts, refs),
        [shape((3, *grid)), shape((3, slots // 128, 128))] + [shape((height, width))] * counts[0],
        (
            total,
            moved,
            free,
            picks,
            cells.reshape(flat),
            wall_rows.reshape(flat),
            slot_angle.reshape(flat),
            wall_count.reshape(1),
            *slab_got,
            *side_got,
        ),
        [VM] * 7 + [SM] + [VM] * sum(counts),
        [pltpu.VMEM((depth * height, width), F32)],
    )
    lam_got = swap_all(slab_rounds, lam_faces)
    part, adj_velocity = call(
        lambda *refs: part_body(counts, refs),
        [shape(grid), shape((3, *grid))],
        (lam, q_in, a_in, *side_got),
        [VM] * (3 + counts[1] + counts[2]),
        [sems((1,))],
        [VM, HB],
    )
    adj_pressure = call(
        lambda *refs: fix_body(refs),
        shape(grid),
        (part, *lam_got),
        [VM] * (1 + counts[0]),
    )
    total = share_and_add(mine, "slab", NROWS // lax.axis_size("slab"))
    total = halve(halve(total, "row"), "col")
    return (adj_pressure, adj_velocity, total)


def solution(mesh):
    in_specs = (
        P("slab", "row", "col"),
        P(None, "slab", "row", "col"),
        P("slab", "row", "col"),
        P("slab", "row", "col"),
        P("slab", "row", "col"),
        P(None, "slab", "row", "col"),
        P("slab", "row", "col"),
        P("slab", "row", "col", None),
        P("slab", "row", "col", None),
        P("slab", "row", "col", None),
        P("slab", "row", "col"),
        P(),
    )
    out_specs = (
        P("slab", "row", "col"),
        P(None, "slab", "row", "col"),
        P(("slab", "row", "col"), None),
    )
    return jax.shard_map(step_back, mesh=mesh, in_specs=in_specs, out_specs=out_specs, check_vma=False)
```

```python
import functools

import jax
import jax.numpy as jnp
from jax import lax
from jax.experimental import pallas as pl
from jax.experimental.pallas import tpu as pltpu
from jax.sharding import PartitionSpec as P


NROWS = 2048
ANG = 64
F32 = jnp.float32
BF16 = jnp.bfloat16
VM = pl.BlockSpec(memory_space=pltpu.VMEM)
HB = pl.BlockSpec(memory_space=pltpu.HBM)
ANY = pl.BlockSpec(memory_space=pl.ANY)
LIMIT = pltpu.CompilerParams(vmem_limit_bytes=24 << 20)


def call(body, outs, args, specs, scratch=(), out_specs=None):
    return pl.pallas_call(
        body,
        out_shape=outs,
        in_specs=specs,
        out_specs=jax.tree.map(lambda _: VM, outs) if out_specs is None else out_specs,
        scratch_shapes=list(scratch),
        compiler_params=LIMIT,
        cost_estimate=pl.CostEstimate(flops=1_000_000, bytes_accessed=1_000_000, transcendentals=0),
    )(*args)


def stay(array):
    return pltpu.with_memory_space_constraint(array, pltpu.HBM)


def fetch(pairs, sems):
    copies = [pltpu.make_async_copy(s, d, sems.at[i]) for i, (s, d) in enumerate(pairs)]
    for copy in copies:
        copy.start()
    return copies


def shape(dims, dtype=F32):
    return jax.ShapeDtypeStruct(tuple(dims), dtype)


def is_odd(axis):
    return lax.rem(lax.axis_index(axis), 2) == 1


def swap_pairs(count, first):
    pairs = []
    for low in range(first, count - 1, 2):
        pairs += [(low, low + 1), (low + 1, low)]
    return pairs


def swap(axis, first, message):
    return lax.ppermute(message, axis, swap_pairs(lax.axis_size(axis), first))


def faces_body(rounds, refs):
    p_ref, k_ref, a_ref = refs[:3]
    outs, (pv_ref, qv_ref, av_ref, kv_ref, sems) = refs[3 : 3 + len(rounds)], refs[3 + len(rounds) :]
    depth = pv_ref.shape[0]
    copies = fetch(((k_ref, kv_ref), (a_ref, av_ref), (p_ref, pv_ref)), sems)
    copies[0].wait()
    copies[1].wait()
    for x in range(depth):
        qv_ref[x] = kv_ref[x] * av_ref[x]
    copies[2].wait()
    odd = is_odd("slab")
    for (_, first), out_ref in zip(rounds, outs):
        at = jnp.where(odd != (first == 1), 0, depth - 1)
        out_ref[0] = pv_ref[at]
        out_ref[1] = qv_ref[at]


def sides_body(rounds, refs):
    pv_ref, qv_ref, t_ref, m_ref = refs[:4]
    outs, (tv_ref, free_ref, mv_ref, sems) = refs[4 : 4 + len(rounds)], refs[4 + len(rounds) :]
    depth, height, width = pv_ref.shape
    copies = fetch(((m_ref, mv_ref), (t_ref, tv_ref)), sems)
    copies[0].wait()
    for x in range(depth):
        free_ref[x] = 1.0 - mv_ref[x].astype(F32)
    copies[1].wait()
    lanes = lax.broadcasted_iota(jnp.int32, (height, width), 1)
    for (axis, first), out_ref in zip(rounds, outs):
        high = is_odd(axis) == (first == 1)
        sign = jnp.where(high, -0.5, 0.5)
        if axis == "row":
            at = jnp.where(high, height - 1, 0)
            inner = jnp.where(high, height - 2, 1)
            for x in range(depth):
                face, second = pl.ds(at, 1), pl.ds(inner, 1)
                free = free_ref[x, face, :]
                out_ref[0, pl.ds(x, 1), :] = pv_ref[x, face, :]
                out_ref[1, pl.ds(x, 1), :] = qv_ref[x, face, :]
                out_ref[2, pl.ds(x, 1), :] = free * (tv_ref[1, x, face, :] + sign * qv_ref[x, second, :])
                out_ref[3, pl.ds(x, 1), :] = free
        else:
            at = jnp.where(high, width - 1, 0)
            turn = jnp.where(high, 1, width - 1)
            table = jnp.zeros((height, width), F32)
            for x in range(depth):
                free, scaled = free_ref[x], qv_ref[x]
                behind = pltpu.roll(scaled, turn, 1)
                fields = (pv_ref[x], scaled, free * (tv_ref[2, x] + sign * behind), free)
                for f, field in enumerate(fields):
                    lane = f * depth + x
                    moved = pltpu.roll(field, lax.rem(lane - at + width, width), 1)
                    table = jnp.where(lanes == lane, moved, table)
            flipped = table.T
            for f in range(4):
                out_ref[f] = flipped[f * depth : (f + 1) * depth]


def take_halo(axis, refs):
    odd = is_odd(axis)
    first = refs[0][...]
    second = refs[1][...] if len(refs) > 1 else jnp.zeros_like(first)
    return jnp.where(odd, first, second), jnp.where(odd, second, first)


def side(field, axis, low, high):
    size = field.shape[axis]
    at = lax.broadcasted_iota(jnp.int32, field.shape, axis)
    upper = jnp.where(at == size - 1, high, pltpu.roll(field, size - 1, axis))
    lower = jnp.where(at == 0, low, pltpu.roll(field, 1, axis))
    return (upper - lower) * 0.5


def halves(value):
    top = value.astype(BF16)
    rest = value - top.astype(F32)
    mid = rest.astype(BF16)
    return top, mid, (rest - mid.astype(F32)).astype(BF16)


def inner_body(pv_ref, qv_ref, tv_ref, v_ref, d_ref, c_ref, r_ref, g_ref, n_ref, s_ref,
               total_ref, moved_ref, pick_ref, cell_ref, row_ref, angle_ref, live_ref,
               vv_ref, dv_ref, count_ref, step_ref, sems):
    depth, _, width = pv_ref.shape
    copies = fetch(
        (
            (s_ref, step_ref),
            (n_ref, count_ref),
            (c_ref, cell_ref),
            (r_ref, row_ref),
            (g_ref, angle_ref),
            (v_ref, vv_ref),
            (d_ref, dv_ref),
        ),
        sems,
    )
    for x in range(depth):
        q = qv_ref[x]
        upper = qv_ref[x + 1] if x + 1 < depth else 0.0
        lower = qv_ref[x - 1] if x > 0 else 0.0
        total_ref[0, x] = tv_ref[0, x] + (upper - lower) * 0.5
        total_ref[1, x] = tv_ref[1, x] + side(q, 0, 0.0, 0.0)
        total_ref[2, x] = tv_ref[2, x] + side(q, 1, 0.0, 0.0)
    for copy in copies[:5]:
        copy.wait()
    line = lax.div(cell_ref[...], width)
    at = lax.broadcasted_iota(jnp.int32, pick_ref.shape, 0)
    pick_ref[...] = jnp.where(at == line, 1.0, 0.0).astype(BF16)
    slot = lax.broadcasted_iota(jnp.int32, live_ref.shape, 1)
    live_ref[...] = jnp.where(slot < count_ref[0], 1, 0)
    turn = lax.rem(step_ref[0], 97).astype(F32) * 0.5
    phase = jnp.cos(jnp.full((8, width), turn, F32))[:1]
    copies[5].wait()
    copies[6].wait()
    for x in range(depth):
        p = pv_ref[x]
        upper = pv_ref[x + 1] if x + 1 < depth else 0.0
        lower = pv_ref[x - 1] if x > 0 else 0.0
        moved_ref[0, x] = vv_ref[0, x] - 0.3 * ((upper - lower) * 0.5) + dv_ref[x] * phase
        moved_ref[1, x] = vv_ref[1, x] - 0.3 * side(p, 0, 0.0, 0.0)
        moved_ref[2, x] = vv_ref[2, x] - 0.3 * side(p, 1, 0.0, 0.0)


def edge_table(low, high, height, width):
    count = low.shape[0]
    lines = []
    for i in range(count):
        lines += [low[i : i + 1], high[i + 1 : i + 2] if i + 1 < count else None]
    lines = [l for l in lines if l is not None]
    fill = jnp.zeros((width - 2 * count, height), F32)
    return jnp.concatenate(lines + [fill, high[:1]], axis=0).T


def main_body(counts, refs):
    total_ref, moved_ref, free_ref, pick_ref, cell_ref, row_ref, angle_ref, live_ref = refs[:8]
    rest = refs[8:]
    n_slab, n_row, n_col = counts
    slab_refs, rest = rest[:n_slab], rest[n_slab:]
    row_refs, rest = rest[:n_row], rest[n_row:]
    col_refs, rest = rest[:n_col], rest[n_col:]
    lam_ref, slot_ref, *face_refs, sens_ref = rest
    _, depth, height, width = total_ref.shape
    slab_low, slab_high = take_halo("slab", slab_refs)
    row_low, row_high = take_halo("row", row_refs)
    col_low, col_high = take_halo("col", col_refs)
    low = jnp.concatenate([col_low[0] * 0.15, col_low[1] * -0.5], axis=0)
    high = jnp.concatenate([col_high[0] * -0.15, col_high[1] * 0.5], axis=0)
    edges = edge_table(low, high, height, width)
    lanes = lax.broadcasted_iota(jnp.int32, (8, width), 1)
    is_edge = (lanes == 0) | (lanes == width - 1)
    tall = lax.broadcasted_iota(jnp.int32, (8, width), 0)
    for x in range(depth):
        for y in range(0, height, 8):
            at = slice(y, y + 8)
            totals = [total_ref[c, x, at] for c in range(3)]
            moves = [moved_ref[c, x, at] for c in range(3)]
            if x == 0:
                totals[0] = totals[0] - 0.5 * slab_low[1, at]
                moves[0] = moves[0] + 0.15 * slab_low[0, at]
            if x == depth - 1:
                totals[0] = totals[0] + 0.5 * slab_high[1, at]
                moves[0] = moves[0] - 0.15 * slab_high[0, at]
            one = slice(x, x + 1)
            if y == 0:
                totals[1] = totals[1] - jnp.where(tall == 0, 0.5 * row_low[1, one], 0.0)
                moves[1] = moves[1] + jnp.where(tall == 0, 0.15 * row_low[0, one], 0.0)
            if y == height - 8:
                totals[1] = totals[1] + jnp.where(tall == 7, 0.5 * row_high[1, one], 0.0)
                moves[1] = moves[1] - jnp.where(tall == 7, 0.15 * row_high[0, one], 0.0)
            for which, terms in ((1, totals), (0, moves)):
                shift = (width - 2 * (which * depth + x)) % width
                turned = pltpu.roll(edges[at], shift, 1) if shift else edges[at]
                terms[2] = terms[2] + jnp.where(is_edge, turned, 0.0)
            free = free_ref[x, at]
            sens = totals[0] * moves[0] + totals[1] * moves[1] + totals[2] * moves[2]
            for c in range(3):
                lam_ref[c, x, at] = free * totals[c]
            sens_ref[pl.ds(x * height + y, 8), :] = -sens
    odd = is_odd("slab")
    for first, face_ref in enumerate(face_refs):
        face_ref[...] = lam_ref[0, jnp.where(odd != (first == 1), 0, depth - 1)]
    cells = cell_ref[...]
    slots = cells.shape[1]
    pieces = jnp.concatenate(halves(sens_ref[...].T), axis=0)
    found = jnp.dot(pieces, pick_ref[...], preferred_element_type=F32)
    found = found[:width] + found[width : 2 * width] + found[2 * width :]
    lane = lax.broadcasted_iota(jnp.int32, (width, slots), 0)
    values = jnp.sum(jnp.where(lane == lax.rem(cells, width), found, 0.0), axis=0, keepdims=True)
    values = jnp.where(live_ref[...] == 1, values, 0.0)
    rows = row_ref[...].astype(F32)
    angles = angle_ref[...]
    for j in range(slots // 128):
        part = slice(128 * j, 128 * (j + 1))
        slot_ref[0, pl.ds(j, 1), :] = values[:, part]
        slot_ref[1, pl.ds(j, 1), :] = rows[:, part]
        slot_ref[2, pl.ds(j, 1), :] = angles[:, part]


def columns(halo, height, width):
    table = jnp.concatenate([halo[2], halo[3]], axis=0)
    table = jnp.concatenate([table, jnp.zeros((width - table.shape[0], height), F32)], axis=0)
    return table.T


def part_body(counts, refs):
    lam_ref, qv_ref, av_ref = refs[:3]
    rest = refs[3:]
    _, n_row, n_col = counts
    row_refs, rest = rest[:n_row], rest[n_row:]
    col_refs, (part_ref, out_ref, sems) = rest[:n_col], rest[n_col:]
    copies = fetch(((lam_ref, out_ref),), sems)
    depth, height, width = av_ref.shape
    row_low, row_high = take_halo("row", row_refs)
    col_low, col_high = (columns(h, height, width) for h in take_halo("col", col_refs))
    for x in range(depth):
        half = 0.5 * qv_ref[x]
        one = slice(x, x + 1)
        free = slice(depth + x, depth + x + 1)
        upper = lam_ref[0, x + 1] if x + 1 < depth else 0.0
        lower = lam_ref[0, x - 1] if x > 0 else 0.0
        row_above = row_high[2, one] - row_high[3, one] * half[height - 1 :]
        row_below = row_low[2, one] + row_low[3, one] * half[:1]
        col_above = col_high[:, one] - col_high[:, free] * half[:, width - 1 :]
        col_below = col_low[:, one] + col_low[:, free] * half[:, :1]
        spread = (
            (upper - lower) * 0.5
            + side(lam_ref[1, x], 0, row_below, row_above)
            + side(lam_ref[2, x], 1, col_below, col_above)
        )
        part_ref[x] = av_ref[x] + 0.3 * spread
    copies[0].wait()


def fix_body(refs):
    part_ref, *face_refs, out_ref = refs
    depth = part_ref.shape[0]
    low, high = take_halo("slab", face_refs)
    for x in range(depth):
        value = part_ref[x]
        if x == 0:
            value = value - 0.15 * low
        if x == depth - 1:
            value = value + 0.15 * high
        out_ref[x] = value


def pack(rows):
    half = rows.shape[0] // 2
    return jnp.concatenate([rows[:half], rows[half:]], axis=1)


def high_side(axis, step):
    return lax.rem(lax.div(lax.axis_index(axis), step), 2) == 1


def split(low, high, mine_high, kept_ref, sent_ref):
    kept_ref[...] = pack(jnp.where(mine_high, high, low))
    sent_ref[...] = pack(jnp.where(mine_high, low, high))


def add_body(parts, kept_ref, got_ref, *out_refs):
    total = kept_ref[...] + got_ref[...]
    low, high = total[:, :ANG], total[:, ANG:]
    if parts is None:
        out_refs[0][...] = jnp.concatenate([low, high], axis=0)
    else:
        split(low, high, high_side(*parts), *out_refs)


def dense_body(block, parts, n_slots, n_prior, refs):
    slot_refs = refs[:n_slots]
    prior = refs[n_slots : n_slots + n_prior]
    *out_refs, pick_ref, piece_ref = refs[n_slots + n_prior :]
    base = (lax.axis_index("slab") * block).astype(F32)
    here = lax.broadcasted_iota(jnp.int32, (block, 128), 0).astype(F32) + base
    knots = lax.broadcasted_iota(jnp.int32, (ANG, 128), 0).astype(F32)
    at = 0
    for slot_ref in slot_refs:
        for d in range(slot_ref.shape[0] // 3):
            for j in range(slot_ref.shape[1]):
                value = slot_ref[3 * d, pl.ds(j, 1), :] * (1.0 / 6.0)
                row = slot_ref[3 * d + 1, pl.ds(j, 1), :]
                angle = slot_ref[3 * d + 2, pl.ds(j, 1), :]
                lanes = pl.ds(at, 128)
                pick_ref[:, lanes] = jnp.where(here == row, 1.0, 0.0).astype(BF16)
                dist = jnp.abs(angle - knots)
                dist = jnp.minimum(dist, ANG - dist)
                outer = jnp.maximum(2.0 - dist, 0.0)
                inner = jnp.maximum(1.0 - dist, 0.0)
                weight = outer * outer * outer - 4.0 * (inner * inner * inner)
                piece_ref[:, lanes] = jnp.concatenate(halves(value * weight), axis=0)
                at += 128
    total = lax.dot_general(
        piece_ref[...], pick_ref[...], (((1,), (1,)), ((), ())), preferred_element_type=F32
    )
    total = (total[:ANG] + total[ANG : 2 * ANG] + total[2 * ANG :]).T
    if prior:
        total = total + prior[0][...]
    if len(out_refs) == 1:
        out_refs[0][...] = total
    else:
        split(total[: block // 2], total[block // 2 :], high_side(*parts), *out_refs)


def dense(block, parts, slots, prior=()):
    count = sum(s.shape[0] // 3 * s.shape[1] * 128 for s in slots)
    packed = shape((block // 4, 2 * ANG))
    return call(
        lambda *refs: dense_body(block, parts, len(slots), len(prior), refs),
        [packed] * 2 if parts else [shape((block, ANG))],
        (*slots, *prior),
        [VM] * (len(slots) + len(prior)),
        [pltpu.VMEM((block, count), BF16), pltpu.VMEM((3 * ANG, count), BF16)],
    )


def share_and_add(slots, axis, block, parts):
    count = lax.axis_size(axis)
    have = slots
    for k in range(count.bit_length() - 1):
        got = lax.ppermute(have, axis, [(i, i ^ (1 << k)) for i in range(count)])
        if 2 << k < count:
            have = jnp.concatenate([have, got], axis=0)
        else:
            total = dense(block, None, (have,))
            return dense(block, parts, (got,), total)


def halve(kept, sent, steps, rows):
    for k, (axis, step) in enumerate(steps):
        count = lax.axis_size(axis)
        got = lax.ppermute(sent, axis, [(i, i ^ step) for i in range(count)])
        following = steps[k + 1] if k + 1 < len(steps) else None
        rows = rows // 2
        outs = [shape((rows // 4, 2 * ANG))] * 2 if following else [shape((rows, ANG))]
        kept, *rest = call(
            functools.partial(add_body, following), outs, (kept, got), [VM] * 2
        )
        if following:
            sent = rest[0]
    return kept


def halving_steps(axis):
    count = lax.axis_size(axis)
    return [(axis, count >> (k + 1)) for k in range(count.bit_length() - 1)]


def rounds_of(axis):
    return [(axis, first) for first in (0, 1) if swap_pairs(lax.axis_size(axis), first)]


def swap_all(rounds, messages):
    got = []
    for (axis, first), message in zip(rounds, messages):
        got.append(swap(axis, first, message))
    return got


def step_back(
    pressure,
    velocity,
    kappa,
    drive,
    adj_pressure_in,
    adj_velocity_in,
    wall_mask,
    wall_cells,
    wall_rows,
    slot_angle,
    wall_count,
    step,
):
    grid = depth, height, width = pressure.shape
    slots = wall_cells.size
    flat = (1, slots)
    sems = pltpu.SemaphoreType.DMA
    slab_rounds, row_rounds, col_rounds = (rounds_of(a) for a in ("slab", "row", "col"))
    side_rounds = row_rounds + col_rounds
    counts = (len(slab_rounds), len(row_rounds), len(col_rounds))

    *faces, p_in, q_in, a_in = call(
        lambda *refs: faces_body(slab_rounds, refs),
        [shape((2, height, width))] * counts[0] + [shape(grid)] * 3,
        (stay(pressure), stay(kappa), stay(adj_pressure_in)),
        [HB] * 3,
        [pltpu.VMEM(grid, F32), sems((3,))],
    )
    slab_got = swap_all(slab_rounds, faces)
    *messages, t_in, free = call(
        lambda *refs: sides_body(side_rounds, refs),
        [shape((4, depth, width if axis == "row" else height)) for axis, _ in side_rounds]
        + [shape((3, *grid)), shape(grid)],
        (p_in, q_in, stay(adj_velocity_in), stay(wall_mask)),
        [VM] * 2 + [HB] * 2,
        [pltpu.VMEM(grid, jnp.int32), sems((2,))],
    )
    side_got = swap_all(side_rounds, messages)
    total, moved, picks, *slot_data = call(
        inner_body,
        [
            shape((3, *grid)),
            shape((3, *grid)),
            shape((depth * height, slots), BF16),
            shape(flat, jnp.int32),
            shape(flat, jnp.int32),
            shape(flat),
            shape(flat, jnp.int32),
        ],
        (
            p_in,
            q_in,
            t_in,
            stay(velocity),
            stay(drive),
            stay(wall_cells.reshape(flat)),
            stay(wall_rows.reshape(flat)),
            stay(slot_angle.reshape(flat)),
            wall_count.reshape(1),
            step,
        ),
        [VM] * 3 + [HB] * 5 + [ANY] * 2,
        [
            pltpu.VMEM((3, *grid), F32),
            pltpu.VMEM(grid, F32),
            pltpu.SMEM((1,), jnp.int32),
            pltpu.SMEM((1,), jnp.int32),
            sems((7,)),
        ],
    )
    lam, mine, *lam_faces = call(
        lambda *refs: main_body(counts, refs),
        [shape((3, *grid)), shape((3, slots // 128, 128))] + [shape((height, width))] * counts[0],
        (
            total,
            moved,
            free,
            picks,
            *slot_data,
            *slab_got,
            *side_got,
        ),
        [VM] * (8 + sum(counts)),
        [pltpu.VMEM((depth * height, width), F32)],
    )
    lam_got = swap_all(slab_rounds, lam_faces)
    part, adj_velocity = call(
        lambda *refs: part_body(counts, refs),
        [shape(grid), shape((3, *grid))],
        (lam, q_in, a_in, *side_got),
        [VM] * (3 + counts[1] + counts[2]),
        [sems((1,))],
        [VM, HB],
    )
    adj_pressure = call(
        lambda *refs: fix_body(refs),
        shape(grid),
        (part, *lam_got),
        [VM] * (1 + counts[0]),
    )
    block = NROWS // lax.axis_size("slab")
    steps = halving_steps("row") + halving_steps("col")
    kept, sent = share_and_add(mine, "slab", block, steps[0])
    total = halve(kept, sent, steps, block)
    return (adj_pressure, adj_velocity, total)


def solution(mesh):
    in_specs = (
        P("slab", "row", "col"),
        P(None, "slab", "row", "col"),
        P("slab", "row", "col"),
        P("slab", "row", "col"),
        P("slab", "row", "col"),
        P(None, "slab", "row", "col"),
        P("slab", "row", "col"),
        P("slab", "row", "col", None),
        P("slab", "row", "col", None),
        P("slab", "row", "col", None),
        P("slab", "row", "col"),
        P(),
    )
    out_specs = (
        P("slab", "row", "col"),
        P(None, "slab", "row", "col"),
        P(("slab", "row", "col"), None),
    )
    return jax.shard_map(step_back, mesh=mesh, in_specs=in_specs, out_specs=out_specs, check_vma=False)
```

```python
import jax
import jax.numpy as jnp
from jax import lax
from jax.experimental import pallas as pl
from jax.experimental.pallas import tpu as pltpu
from jax.sharding import PartitionSpec as P


NROWS = 2048
ANG = 64
F32 = jnp.float32
BF16 = jnp.bfloat16
VM = pl.BlockSpec(memory_space=pltpu.VMEM)
SM = pl.BlockSpec(memory_space=pltpu.SMEM)
HB = pl.BlockSpec(memory_space=pltpu.HBM)
LIMIT = pltpu.CompilerParams(vmem_limit_bytes=24 << 20)


def call(body, outs, args, specs, scratch=(), out_specs=None):
    return pl.pallas_call(
        body,
        out_shape=outs,
        in_specs=specs,
        out_specs=jax.tree.map(lambda _: VM, outs) if out_specs is None else out_specs,
        scratch_shapes=list(scratch),
        compiler_params=LIMIT,
        cost_estimate=pl.CostEstimate(flops=1_000_000, bytes_accessed=1_000_000, transcendentals=0),
    )(*args)


def stay(array):
    return pltpu.with_memory_space_constraint(array, pltpu.HBM)


def fetch(pairs, sems):
    copies = [pltpu.make_async_copy(s, d, sems.at[i]) for i, (s, d) in enumerate(pairs)]
    for copy in copies:
        copy.start()
    return copies


def shape(dims, dtype=F32):
    return jax.ShapeDtypeStruct(tuple(dims), dtype)


def is_odd(axis):
    return lax.rem(lax.axis_index(axis), 2) == 1


def swap_pairs(count, first):
    pairs = []
    for low in range(first, count - 1, 2):
        pairs += [(low, low + 1), (low + 1, low)]
    return pairs


def swap(axis, first, message):
    return lax.ppermute(message, axis, swap_pairs(lax.axis_size(axis), first))


def faces_body(rounds, refs):
    p_ref, k_ref, a_ref, m_ref, c_ref, r_ref, g_ref = refs[:7]
    outs, rest = refs[7 : 7 + len(rounds)], refs[7 + len(rounds) :]
    pv_ref, qv_ref, av_ref, free_ref, cell_ref, row_ref, angle_ref = rest[:7]
    kv_ref, mv_ref, sems = rest[7:]
    depth = pv_ref.shape[0]
    copies = fetch(
        (
            (k_ref, kv_ref),
            (a_ref, av_ref),
            (p_ref, pv_ref),
            (m_ref, mv_ref),
            (c_ref, cell_ref),
            (r_ref, row_ref),
            (g_ref, angle_ref),
        ),
        sems,
    )
    copies[0].wait()
    copies[1].wait()
    for x in range(depth):
        qv_ref[x] = kv_ref[x] * av_ref[x]
    copies[2].wait()
    odd = is_odd("slab")
    for (_, first), out_ref in zip(rounds, outs):
        at = jnp.where(odd != (first == 1), 0, depth - 1)
        out_ref[0] = pv_ref[at]
        out_ref[1] = qv_ref[at]
    copies[3].wait()
    for x in range(depth):
        free_ref[x] = 1.0 - mv_ref[x].astype(F32)
    for copy in copies[4:]:
        copy.wait()


def sides_body(rounds, refs):
    pv_ref, qv_ref, tv_ref, free_ref, *outs = refs
    depth, height, width = pv_ref.shape
    lanes = lax.broadcasted_iota(jnp.int32, (height, width), 1)
    for (axis, first), out_ref in zip(rounds, outs):
        high = is_odd(axis) == (first == 1)
        sign = jnp.where(high, -0.5, 0.5)
        if axis == "row":
            at = jnp.where(high, height - 1, 0)
            inner = jnp.where(high, height - 2, 1)
            for x in range(depth):
                face, second = pl.ds(at, 1), pl.ds(inner, 1)
                free = free_ref[x, face, :]
                out_ref[0, pl.ds(x, 1), :] = pv_ref[x, face, :]
                out_ref[1, pl.ds(x, 1), :] = qv_ref[x, face, :]
                out_ref[2, pl.ds(x, 1), :] = free * (tv_ref[1, x, face, :] + sign * qv_ref[x, second, :])
                out_ref[3, pl.ds(x, 1), :] = free
        else:
            at = jnp.where(high, width - 1, 0)
            turn = jnp.where(high, 1, width - 1)
            table = jnp.zeros((height, width), F32)
            for x in range(depth):
                free, scaled = free_ref[x], qv_ref[x]
                behind = pltpu.roll(scaled, turn, 1)
                fields = (pv_ref[x], scaled, free * (tv_ref[2, x] + sign * behind), free)
                for f, field in enumerate(fields):
                    lane = f * depth + x
                    moved = pltpu.roll(field, lax.rem(lane - at + width, width), 1)
                    table = jnp.where(lanes == lane, moved, table)
            flipped = table.T
            for f in range(4):
                out_ref[f] = flipped[f * depth : (f + 1) * depth]


def take_halo(axis, refs):
    odd = is_odd(axis)
    first = refs[0][...]
    second = refs[1][...] if len(refs) > 1 else jnp.zeros_like(first)
    return jnp.where(odd, first, second), jnp.where(odd, second, first)


def side(field, axis, low, high):
    size = field.shape[axis]
    at = lax.broadcasted_iota(jnp.int32, field.shape, axis)
    upper = jnp.where(at == size - 1, high, pltpu.roll(field, size - 1, axis))
    lower = jnp.where(at == 0, low, pltpu.roll(field, 1, axis))
    return (upper - lower) * 0.5


def halves(value):
    top = value.astype(BF16)
    rest = value - top.astype(F32)
    mid = rest.astype(BF16)
    return top, mid, (rest - mid.astype(F32)).astype(BF16)


def inner_body(pv_ref, qv_ref, tv_ref, v_ref, d_ref, cell_ref, step_ref, count_ref, total_ref, moved_ref, pick_ref, live_ref):
    depth, _, width = pv_ref.shape
    line = lax.div(cell_ref[...], width)
    at = lax.broadcasted_iota(jnp.int32, pick_ref.shape, 0)
    pick_ref[...] = jnp.where(at == line, 1.0, 0.0).astype(BF16)
    slot = lax.broadcasted_iota(jnp.int32, live_ref.shape, 1)
    live_ref[...] = jnp.where(slot < count_ref[0], 1, 0)
    turn = lax.rem(step_ref[0], 97).astype(F32) * 0.5
    phase = jnp.cos(jnp.full((8, width), turn, F32))[:1]
    for x in range(depth):
        p, q = pv_ref[x], qv_ref[x]

        def along(field, ref):
            upper = ref[x + 1] if x + 1 < depth else 0.0
            lower = ref[x - 1] if x > 0 else 0.0
            return (upper - lower) * 0.5, side(field, 0, 0.0, 0.0), side(field, 1, 0.0, 0.0)

        for comp, (slope, gain) in enumerate(zip(along(p, pv_ref), along(q, qv_ref))):
            total_ref[comp, x] = tv_ref[comp, x] + gain
            moved = v_ref[comp, x] - 0.3 * slope
            moved_ref[comp, x] = moved + d_ref[x] * phase if comp == 0 else moved


def edge_table(low, high, height, width):
    count = low.shape[0]
    lines = []
    for i in range(count):
        lines += [low[i : i + 1], high[i + 1 : i + 2] if i + 1 < count else None]
    lines = [l for l in lines if l is not None]
    fill = jnp.zeros((width - 2 * count, height), F32)
    return jnp.concatenate(lines + [fill, high[:1]], axis=0).T


def main_body(counts, refs):
    total_ref, moved_ref, free_ref, pick_ref, cell_ref, row_ref, angle_ref, live_ref = refs[:8]
    rest = refs[8:]
    n_slab, n_row, n_col = counts
    slab_refs, rest = rest[:n_slab], rest[n_slab:]
    row_refs, rest = rest[:n_row], rest[n_row:]
    col_refs, rest = rest[:n_col], rest[n_col:]
    lam_ref, slot_ref, *face_refs, sens_ref = rest
    _, depth, height, width = total_ref.shape
    slab_low, slab_high = take_halo("slab", slab_refs)
    row_low, row_high = take_halo("row", row_refs)
    col_low, col_high = take_halo("col", col_refs)
    low = jnp.concatenate([col_low[0] * 0.15, col_low[1] * -0.5], axis=0)
    high = jnp.concatenate([col_high[0] * -0.15, col_high[1] * 0.5], axis=0)
    edges = edge_table(low, high, height, width)
    lanes = lax.broadcasted_iota(jnp.int32, (8, width), 1)
    is_edge = (lanes == 0) | (lanes == width - 1)
    tall = lax.broadcasted_iota(jnp.int32, (8, width), 0)
    for x in range(depth):
        for y in range(0, height, 8):
            at = slice(y, y + 8)
            totals = [total_ref[c, x, at] for c in range(3)]
            moves = [moved_ref[c, x, at] for c in range(3)]
            if x == 0:
                totals[0] = totals[0] - 0.5 * slab_low[1, at]
                moves[0] = moves[0] + 0.15 * slab_low[0, at]
            if x == depth - 1:
                totals[0] = totals[0] + 0.5 * slab_high[1, at]
                moves[0] = moves[0] - 0.15 * slab_high[0, at]
            one = slice(x, x + 1)
            if y == 0:
                totals[1] = totals[1] - jnp.where(tall == 0, 0.5 * row_low[1, one], 0.0)
                moves[1] = moves[1] + jnp.where(tall == 0, 0.15 * row_low[0, one], 0.0)
            if y == height - 8:
                totals[1] = totals[1] + jnp.where(tall == 7, 0.5 * row_high[1, one], 0.0)
                moves[1] = moves[1] - jnp.where(tall == 7, 0.15 * row_high[0, one], 0.0)
            for which, terms in ((1, totals), (0, moves)):
                shift = (width - 2 * (which * depth + x)) % width
                turned = pltpu.roll(edges[at], shift, 1) if shift else edges[at]
                terms[2] = terms[2] + jnp.where(is_edge, turned, 0.0)
            free = free_ref[x, at]
            sens = totals[0] * moves[0] + totals[1] * moves[1] + totals[2] * moves[2]
            for c in range(3):
                lam_ref[c, x, at] = free * totals[c]
            sens_ref[pl.ds(x * height + y, 8), :] = -sens
    odd = is_odd("slab")
    for first, face_ref in enumerate(face_refs):
        face_ref[...] = lam_ref[0, jnp.where(odd != (first == 1), 0, depth - 1)]
    cells = cell_ref[...]
    slots = cells.shape[1]
    pieces = jnp.concatenate(halves(sens_ref[...].T), axis=0)
    found = jnp.dot(pieces, pick_ref[...], preferred_element_type=F32)
    found = found[:width] + found[width : 2 * width] + found[2 * width :]
    lane = lax.broadcasted_iota(jnp.int32, (width, slots), 0)
    values = jnp.sum(jnp.where(lane == lax.rem(cells, width), found, 0.0), axis=0, keepdims=True)
    values = jnp.where(live_ref[...] == 1, values, 0.0)
    rows = row_ref[...].astype(F32)
    angles = angle_ref[...]
    for j in range(slots // 128):
        part = slice(128 * j, 128 * (j + 1))
        slot_ref[0, pl.ds(j, 1), :] = values[:, part]
        slot_ref[1, pl.ds(j, 1), :] = rows[:, part]
        slot_ref[2, pl.ds(j, 1), :] = angles[:, part]


def columns(halo, height, width):
    table = jnp.concatenate([halo[2], halo[3]], axis=0)
    table = jnp.concatenate([table, jnp.zeros((width - table.shape[0], height), F32)], axis=0)
    return table.T


def part_body(counts, refs):
    lam_ref, qv_ref, av_ref = refs[:3]
    rest = refs[3:]
    _, n_row, n_col = counts
    row_refs, rest = rest[:n_row], rest[n_row:]
    col_refs, (part_ref, out_ref, sems) = rest[:n_col], rest[n_col:]
    copies = fetch(((lam_ref, out_ref),), sems)
    depth, height, width = av_ref.shape
    row_low, row_high = take_halo("row", row_refs)
    col_low, col_high = (columns(h, height, width) for h in take_halo("col", col_refs))
    for x in range(depth):
        half = 0.5 * qv_ref[x]
        one = slice(x, x + 1)
        free = slice(depth + x, depth + x + 1)
        upper = lam_ref[0, x + 1] if x + 1 < depth else 0.0
        lower = lam_ref[0, x - 1] if x > 0 else 0.0
        row_above = row_high[2, one] - row_high[3, one] * half[height - 1 :]
        row_below = row_low[2, one] + row_low[3, one] * half[:1]
        col_above = col_high[:, one] - col_high[:, free] * half[:, width - 1 :]
        col_below = col_low[:, one] + col_low[:, free] * half[:, :1]
        spread = (
            (upper - lower) * 0.5
            + side(lam_ref[1, x], 0, row_below, row_above)
            + side(lam_ref[2, x], 1, col_below, col_above)
        )
        part_ref[x] = av_ref[x] + 0.3 * spread
    copies[0].wait()


def fix_body(refs):
    part_ref, *face_refs, out_ref = refs
    depth = part_ref.shape[0]
    low, high = take_halo("slab", face_refs)
    for x in range(depth):
        value = part_ref[x]
        if x == 0:
            value = value - 0.15 * low
        if x == depth - 1:
            value = value + 0.15 * high
        out_ref[x] = value


def pack(rows):
    half = rows.shape[0] // 2
    return jnp.concatenate([rows[:half], rows[half:]], axis=1)


def add_body(*refs):
    *parts, out_ref = refs
    total = parts[0][...]
    for part in parts[1:]:
        total = total + part[...]
    out_ref[...] = jnp.concatenate([total[:, :ANG], total[:, ANG:]], axis=0)


def dense_body(block, group, n_slots, n_prior, refs):
    slot_refs = refs[:n_slots]
    prior = refs[n_slots : n_slots + n_prior]
    *out_refs, pick_ref, piece_ref = refs[n_slots + n_prior : len(refs) - bool(group)]
    base = (lax.axis_index("slab") * block).astype(F32)
    here = lax.broadcasted_iota(jnp.int32, (block, 128), 0).astype(F32) + base
    knots = lax.broadcasted_iota(jnp.int32, (ANG, 128), 0).astype(F32)
    at = 0
    for slot_ref in slot_refs:
        for d in range(slot_ref.shape[0] // 3):
            for j in range(slot_ref.shape[1]):
                value = slot_ref[3 * d, pl.ds(j, 1), :] * (1.0 / 6.0)
                row = slot_ref[3 * d + 1, pl.ds(j, 1), :]
                angle = slot_ref[3 * d + 2, pl.ds(j, 1), :]
                lanes = pl.ds(at, 128)
                pick_ref[:, lanes] = jnp.where(here == row, 1.0, 0.0).astype(BF16)
                dist = jnp.abs(angle - knots)
                dist = jnp.minimum(dist, ANG - dist)
                outer = jnp.maximum(2.0 - dist, 0.0)
                inner = jnp.maximum(1.0 - dist, 0.0)
                weight = outer * outer * outer - 4.0 * (inner * inner * inner)
                piece_ref[:, lanes] = jnp.concatenate(halves(value * weight), axis=0)
                at += 128
    total = lax.dot_general(
        piece_ref[...], pick_ref[...], (((1,), (1,)), ((), ())), preferred_element_type=F32
    )
    total = (total[:ANG] + total[ANG : 2 * ANG] + total[2 * ANG :]).T
    if prior:
        total = total + prior[0][...]
    if group is None:
        out_refs[0][...] = total
    else:
        total_ref = refs[-1]
        rows = block // len(out_refs)
        for i in range(len(out_refs)):
            total_ref[i] = pack(total[i * rows : (i + 1) * rows])
        me = lax.axis_index(group)
        for i, out_ref in enumerate(out_refs):
            out_ref[...] = total_ref[lax.bitwise_xor(me, i)]


def dense(block, group, slots, prior=()):
    count = sum(s.shape[0] // 3 * s.shape[1] * 128 for s in slots)
    members = lax.axis_size(group) if group else 1
    packed = (block // members // 2, 2 * ANG)
    return call(
        lambda *refs: dense_body(block, group, len(slots), len(prior), refs),
        [shape(packed)] * members if group else [shape((block, ANG))],
        (*slots, *prior),
        [VM] * (len(slots) + len(prior)),
        [pltpu.VMEM((block, count), BF16), pltpu.VMEM((3 * ANG, count), BF16)]
        + ([pltpu.VMEM((members, *packed), F32)] if group else []),
    )


def share_and_add(slots, axis, block, group):
    count = lax.axis_size(axis)
    have = slots
    for k in range(count.bit_length() - 1):
        got = lax.ppermute(have, axis, [(i, i ^ (1 << k)) for i in range(count)])
        if 2 << k < count:
            have = jnp.concatenate([have, got], axis=0)
        else:
            total = dense(block, None, (have,))
            return dense(block, group, (got,), total)


def collect(sums, group):
    count = lax.axis_size(group)
    parts = [sums[0]]
    for i in range(1, count):
        parts.append(lax.ppermute(sums[i], group, [(j, j ^ i) for j in range(count)]))
    return call(add_body, shape((2 * sums[0].shape[0], ANG)), parts, [VM] * count)


def rounds_of(axis):
    return [(axis, first) for first in (0, 1) if swap_pairs(lax.axis_size(axis), first)]


def swap_all(rounds, messages):
    got = []
    for (axis, first), message in zip(rounds, messages):
        got.append(swap(axis, first, message))
    return got


def step_back(
    pressure,
    velocity,
    kappa,
    drive,
    adj_pressure_in,
    adj_velocity_in,
    wall_mask,
    wall_cells,
    wall_rows,
    slot_angle,
    wall_count,
    step,
):
    grid = depth, height, width = pressure.shape
    slots = wall_cells.size
    flat = (1, slots)
    sems = pltpu.SemaphoreType.DMA
    slab_rounds, row_rounds, col_rounds = (rounds_of(a) for a in ("slab", "row", "col"))
    side_rounds = row_rounds + col_rounds
    counts = (len(slab_rounds), len(row_rounds), len(col_rounds))

    outs = call(
        lambda *refs: faces_body(slab_rounds, refs),
        [shape((2, height, width))] * counts[0]
        + [shape(grid)] * 4
        + [shape(flat, jnp.int32), shape(flat, jnp.int32), shape(flat)],
        (
            *(stay(x) for x in (pressure, kappa, adj_pressure_in, wall_mask)),
            *(stay(x.reshape(flat)) for x in (wall_cells, wall_rows, slot_angle)),
        ),
        [HB] * 7,
        [pltpu.VMEM(grid, F32), pltpu.VMEM(grid, jnp.int32), sems((7,))],
    )
    faces, (p_in, q_in, a_in, free, *slot_data) = outs[: counts[0]], outs[counts[0] :]
    slab_got = swap_all(slab_rounds, faces)
    messages = call(
        lambda *refs: sides_body(side_rounds, refs),
        [shape((4, depth, width if axis == "row" else height)) for axis, _ in side_rounds],
        (p_in, q_in, adj_velocity_in, free),
        [VM] * 4,
    )
    side_got = swap_all(side_rounds, messages)
    total, moved, picks, live = call(
        inner_body,
        [
            shape((3, *grid)),
            shape((3, *grid)),
            shape((depth * height, slots), BF16),
            shape(flat, jnp.int32),
        ],
        (p_in, q_in, adj_velocity_in, velocity, drive, slot_data[0], step, wall_count.reshape(1)),
        [VM] * 6 + [SM] * 2,
    )
    lam, mine, *lam_faces = call(
        lambda *refs: main_body(counts, refs),
        [shape((3, *grid)), shape((3, slots // 128, 128))] + [shape((height, width))] * counts[0],
        (
            total,
            moved,
            free,
            picks,
            *slot_data,
            live,
            *slab_got,
            *side_got,
        ),
        [VM] * (8 + sum(counts)),
        [pltpu.VMEM((depth * height, width), F32)],
    )
    lam_got = swap_all(slab_rounds, lam_faces)
    part, adj_velocity = call(
        lambda *refs: part_body(counts, refs),
        [shape(grid), shape((3, *grid))],
        (lam, q_in, a_in, *side_got),
        [VM] * (3 + counts[1] + counts[2]),
        [sems((1,))],
        [VM, HB],
    )
    adj_pressure = call(
        lambda *refs: fix_body(refs),
        shape(grid),
        (part, *lam_got),
        [VM] * (1 + counts[0]),
    )
    block = NROWS // lax.axis_size("slab")
    group = ("row", "col")
    total = collect(share_and_add(mine, "slab", block, group), group)
    return (adj_pressure, adj_velocity, total)


def solution(mesh):
    in_specs = (
        P("slab", "row", "col"),
        P(None, "slab", "row", "col"),
        P("slab", "row", "col"),
        P("slab", "row", "col"),
        P("slab", "row", "col"),
        P(None, "slab", "row", "col"),
        P("slab", "row", "col"),
        P("slab", "row", "col", None),
        P("slab", "row", "col", None),
        P("slab", "row", "col", None),
        P("slab", "row", "col"),
        P(),
    )
    out_specs = (
        P("slab", "row", "col"),
        P(None, "slab", "row", "col"),
        P(("slab", "row", "col"), None),
    )
    return jax.shard_map(step_back, mesh=mesh, in_specs=in_specs, out_specs=out_specs, check_vma=False)
```

```python
import jax
import jax.numpy as jnp
from jax import lax
from jax.experimental import pallas as pl
from jax.experimental.pallas import tpu as pltpu
from jax.sharding import PartitionSpec as P


NROWS = 2048
ANG = 64
F32 = jnp.float32
BF16 = jnp.bfloat16
VM = pl.BlockSpec(memory_space=pltpu.VMEM)
SM = pl.BlockSpec(memory_space=pltpu.SMEM)
HB = pl.BlockSpec(memory_space=pltpu.HBM)
LIMIT = pltpu.CompilerParams(vmem_limit_bytes=24 << 20)


def call(body, outs, args, specs, scratch=(), out_specs=None):
    return pl.pallas_call(
        body,
        out_shape=outs,
        in_specs=specs,
        out_specs=jax.tree.map(lambda _: VM, outs) if out_specs is None else out_specs,
        scratch_shapes=list(scratch),
        compiler_params=LIMIT,
        cost_estimate=pl.CostEstimate(flops=1_000_000, bytes_accessed=1_000_000, transcendentals=0),
    )(*args)


def stay(array):
    return pltpu.with_memory_space_constraint(array, pltpu.HBM)


def fetch(pairs, sems):
    copies = [pltpu.make_async_copy(s, d, sems.at[i]) for i, (s, d) in enumerate(pairs)]
    for copy in copies:
        copy.start()
    return copies


def shape(dims, dtype=F32):
    return jax.ShapeDtypeStruct(tuple(dims), dtype)


def is_odd(axis):
    return lax.rem(lax.axis_index(axis), 2) == 1


def swap_pairs(count, first):
    pairs = []
    for low in range(first, count - 1, 2):
        pairs += [(low, low + 1), (low + 1, low)]
    return pairs


def swap(axis, first, message):
    count, lines = lax.axis_size(axis), lax.axis_size("row")
    pairs = swap_pairs(count, first)
    if axis != "slab" or lines % 2:
        return lax.ppermute(message, axis, pairs)
    left = set(range(count)) - {i for i, _ in pairs}
    both = [(i * lines + r, j * lines + r) for i, j in pairs for r in range(lines)]
    both += [(i * lines + r, i * lines + (r ^ 1)) for i in sorted(left) for r in range(lines)]
    return lax.ppermute(message, (axis, "row"), both)


def faces_body(rounds, refs):
    p_ref, k_ref, a_ref, m_ref = refs[:4]
    outs, rest = refs[4 : 4 + len(rounds)], refs[4 + len(rounds) :]
    pv_ref, qv_ref, av_ref, free_ref, kv_ref, mv_ref, sems = rest
    depth = pv_ref.shape[0]
    copies = fetch(((k_ref, kv_ref), (a_ref, av_ref), (p_ref, pv_ref), (m_ref, mv_ref)), sems)
    copies[0].wait()
    copies[1].wait()
    for x in range(depth):
        qv_ref[x] = kv_ref[x] * av_ref[x]
    copies[2].wait()
    odd = is_odd("slab")
    for (_, first), out_ref in zip(rounds, outs):
        at = jnp.where(odd != (first == 1), 0, depth - 1)
        out_ref[0] = pv_ref[at]
        out_ref[1] = qv_ref[at]
    copies[3].wait()
    for x in range(depth):
        free_ref[x] = 1.0 - mv_ref[x].astype(F32)


def sides_body(rounds, refs):
    pv_ref, qv_ref, tv_ref, free_ref, *outs = refs
    depth, height, width = pv_ref.shape
    lanes = lax.broadcasted_iota(jnp.int32, (height, width), 1)
    for (axis, first), out_ref in zip(rounds, outs):
        high = is_odd(axis) == (first == 1)
        sign = jnp.where(high, -0.5, 0.5)
        if axis == "row":
            at = jnp.where(high, height - 1, 0)
            inner = jnp.where(high, height - 2, 1)
            for x in range(depth):
                face, second = pl.ds(at, 1), pl.ds(inner, 1)
                free = free_ref[x, face, :]
                out_ref[0, pl.ds(x, 1), :] = pv_ref[x, face, :]
                out_ref[1, pl.ds(x, 1), :] = qv_ref[x, face, :]
                out_ref[2, pl.ds(x, 1), :] = free * (tv_ref[1, x, face, :] + sign * qv_ref[x, second, :])
                out_ref[3, pl.ds(x, 1), :] = free
        else:
            at = jnp.where(high, width - 1, 0)
            turn = jnp.where(high, 1, width - 1)
            table = jnp.zeros((height, width), F32)
            for x in range(depth):
                free, scaled = free_ref[x], qv_ref[x]
                behind = pltpu.roll(scaled, turn, 1)
                fields = (pv_ref[x], scaled, free * (tv_ref[2, x] + sign * behind), free)
                for f, field in enumerate(fields):
                    lane = f * depth + x
                    moved = pltpu.roll(field, lax.rem(lane - at + width, width), 1)
                    table = jnp.where(lanes == lane, moved, table)
            flipped = table.T
            for f in range(4):
                out_ref[f] = flipped[f * depth : (f + 1) * depth]


def take_halo(axis, refs):
    odd = is_odd(axis)
    first = refs[0][...]
    second = refs[1][...] if len(refs) > 1 else jnp.zeros_like(first)
    me = lax.axis_index(axis)
    low, high = jnp.where(odd, first, second), jnp.where(odd, second, first)
    return jnp.where(me == 0, 0.0, low), jnp.where(me == lax.axis_size(axis) - 1, 0.0, high)


def side(field, axis, low, high):
    size = field.shape[axis]
    at = lax.broadcasted_iota(jnp.int32, field.shape, axis)
    upper = jnp.where(at == size - 1, high, pltpu.roll(field, size - 1, axis))
    lower = jnp.where(at == 0, low, pltpu.roll(field, 1, axis))
    return (upper - lower) * 0.5


def halves(value):
    top = value.astype(BF16)
    rest = value - top.astype(F32)
    mid = rest.astype(BF16)
    return top, mid, (rest - mid.astype(F32)).astype(BF16)


def inner_body(pv_ref, qv_ref, tv_ref, v_ref, d_ref, c_ref, r_ref, g_ref, step_ref, count_ref,
               total_ref, moved_ref, pick_ref, cell_ref, row_ref, angle_ref, live_ref, sems):
    depth, _, width = pv_ref.shape
    copies = fetch(((c_ref, cell_ref), (r_ref, row_ref), (g_ref, angle_ref)), sems)
    slot = lax.broadcasted_iota(jnp.int32, live_ref.shape, 1)
    live_ref[...] = jnp.where(slot < count_ref[0], 1, 0)
    turn = lax.rem(step_ref[0], 97).astype(F32) * 0.5
    phase = jnp.cos(jnp.full((8, width), turn, F32))[:1]
    for x in range(depth):
        p, q = pv_ref[x], qv_ref[x]

        def along(field, ref):
            upper = ref[x + 1] if x + 1 < depth else 0.0
            lower = ref[x - 1] if x > 0 else 0.0
            return (upper - lower) * 0.5, side(field, 0, 0.0, 0.0), side(field, 1, 0.0, 0.0)

        for comp, (slope, gain) in enumerate(zip(along(p, pv_ref), along(q, qv_ref))):
            total_ref[comp, x] = tv_ref[comp, x] + gain
            moved = v_ref[comp, x] - 0.3 * slope
            moved_ref[comp, x] = moved + d_ref[x] * phase if comp == 0 else moved
    for copy in copies:
        copy.wait()
    line = lax.div(cell_ref[...], width)
    at = lax.broadcasted_iota(jnp.int32, pick_ref.shape, 0)
    pick_ref[...] = jnp.where(at == line, 1.0, 0.0).astype(BF16)


def edge_table(low, high, height, width):
    count = low.shape[0]
    lines = []
    for i in range(count):
        lines += [low[i : i + 1], high[i + 1 : i + 2] if i + 1 < count else None]
    lines = [l for l in lines if l is not None]
    fill = jnp.zeros((width - 2 * count, height), F32)
    return jnp.concatenate(lines + [fill, high[:1]], axis=0).T


def main_body(counts, refs):
    total_ref, moved_ref, free_ref, pick_ref, cell_ref, row_ref, angle_ref, live_ref = refs[:8]
    rest = refs[8:]
    n_slab, n_row, n_col = counts
    slab_refs, rest = rest[:n_slab], rest[n_slab:]
    row_refs, rest = rest[:n_row], rest[n_row:]
    col_refs, rest = rest[:n_col], rest[n_col:]
    lam_ref, slot_ref, *face_refs, sens_ref = rest
    _, depth, height, width = total_ref.shape
    slab_low, slab_high = take_halo("slab", slab_refs)
    row_low, row_high = take_halo("row", row_refs)
    col_low, col_high = take_halo("col", col_refs)
    low = jnp.concatenate([col_low[0] * 0.15, col_low[1] * -0.5], axis=0)
    high = jnp.concatenate([col_high[0] * -0.15, col_high[1] * 0.5], axis=0)
    edges = edge_table(low, high, height, width)
    lanes = lax.broadcasted_iota(jnp.int32, (8, width), 1)
    is_edge = (lanes == 0) | (lanes == width - 1)
    tall = lax.broadcasted_iota(jnp.int32, (8, width), 0)
    for x in range(depth):
        for y in range(0, height, 8):
            at = slice(y, y + 8)
            totals = [total_ref[c, x, at] for c in range(3)]
            moves = [moved_ref[c, x, at] for c in range(3)]
            if x == 0:
                totals[0] = totals[0] - 0.5 * slab_low[1, at]
                moves[0] = moves[0] + 0.15 * slab_low[0, at]
            if x == depth - 1:
                totals[0] = totals[0] + 0.5 * slab_high[1, at]
                moves[0] = moves[0] - 0.15 * slab_high[0, at]
            one = slice(x, x + 1)
            if y == 0:
                totals[1] = totals[1] - jnp.where(tall == 0, 0.5 * row_low[1, one], 0.0)
                moves[1] = moves[1] + jnp.where(tall == 0, 0.15 * row_low[0, one], 0.0)
            if y == height - 8:
                totals[1] = totals[1] + jnp.where(tall == 7, 0.5 * row_high[1, one], 0.0)
                moves[1] = moves[1] - jnp.where(tall == 7, 0.15 * row_high[0, one], 0.0)
            for which, terms in ((1, totals), (0, moves)):
                shift = (width - 2 * (which * depth + x)) % width
                turned = pltpu.roll(edges[at], shift, 1) if shift else edges[at]
                terms[2] = terms[2] + jnp.where(is_edge, turned, 0.0)
            free = free_ref[x, at]
            sens = totals[0] * moves[0] + totals[1] * moves[1] + totals[2] * moves[2]
            for c in range(3):
                lam_ref[c, x, at] = free * totals[c]
            sens_ref[pl.ds(x * height + y, 8), :] = -sens
    odd = is_odd("slab")
    for first, face_ref in enumerate(face_refs):
        face_ref[...] = lam_ref[0, jnp.where(odd != (first == 1), 0, depth - 1)]
    cells = cell_ref[...]
    slots = cells.shape[1]
    pieces = jnp.concatenate(halves(sens_ref[...].T), axis=0)
    found = jnp.dot(pieces, pick_ref[...], preferred_element_type=F32)
    found = found[:width] + found[width : 2 * width] + found[2 * width :]
    lane = lax.broadcasted_iota(jnp.int32, (width, slots), 0)
    values = jnp.sum(jnp.where(lane == lax.rem(cells, width), found, 0.0), axis=0, keepdims=True)
    values = jnp.where(live_ref[...] == 1, values, 0.0)
    rows = row_ref[...].astype(F32)
    angles = angle_ref[...]
    for j in range(slots // 128):
        part = slice(128 * j, 128 * (j + 1))
        slot_ref[0, pl.ds(j, 1), :] = values[:, part]
        slot_ref[1, pl.ds(j, 1), :] = rows[:, part]
        slot_ref[2, pl.ds(j, 1), :] = angles[:, part]


def columns(halo, height, width):
    table = jnp.concatenate([halo[2], halo[3]], axis=0)
    table = jnp.concatenate([table, jnp.zeros((width - table.shape[0], height), F32)], axis=0)
    return table.T


def part_body(counts, refs):
    lam_ref, qv_ref, av_ref = refs[:3]
    rest = refs[3:]
    _, n_row, n_col = counts
    row_refs, rest = rest[:n_row], rest[n_row:]
    col_refs, (part_ref, out_ref, sems) = rest[:n_col], rest[n_col:]
    copies = fetch(((lam_ref, out_ref),), sems)
    depth, height, width = av_ref.shape
    row_low, row_high = take_halo("row", row_refs)
    col_low, col_high = (columns(h, height, width) for h in take_halo("col", col_refs))
    for x in range(depth):
        half = 0.5 * qv_ref[x]
        one = slice(x, x + 1)
        free = slice(depth + x, depth + x + 1)
        upper = lam_ref[0, x + 1] if x + 1 < depth else 0.0
        lower = lam_ref[0, x - 1] if x > 0 else 0.0
        row_above = row_high[2, one] - row_high[3, one] * half[height - 1 :]
        row_below = row_low[2, one] + row_low[3, one] * half[:1]
        col_above = col_high[:, one] - col_high[:, free] * half[:, width - 1 :]
        col_below = col_low[:, one] + col_low[:, free] * half[:, :1]
        spread = (
            (upper - lower) * 0.5
            + side(lam_ref[1, x], 0, row_below, row_above)
            + side(lam_ref[2, x], 1, col_below, col_above)
        )
        part_ref[x] = av_ref[x] + 0.3 * spread
    copies[0].wait()


def fix_body(refs):
    part_ref, *face_refs, out_ref = refs
    depth = part_ref.shape[0]
    low, high = take_halo("slab", face_refs)
    for x in range(depth):
        value = part_ref[x]
        if x == 0:
            value = value - 0.15 * low
        if x == depth - 1:
            value = value + 0.15 * high
        out_ref[x] = value


def pack(rows):
    half = rows.shape[0] // 2
    return jnp.concatenate([rows[:half], rows[half:]], axis=1)


def add_body(*refs):
    *parts, out_ref = refs
    total = parts[0][...]
    for part in parts[1:]:
        total = total + part[...]
    out_ref[...] = jnp.concatenate([total[:, :ANG], total[:, ANG:]], axis=0)


def four_weights(angle):
    below = jnp.floor(angle)
    f = angle - below
    g = 1.0 - f
    f3, g3 = f * f * f, g * g * g
    f1, g1 = 1.0 + f, 1.0 + g
    weights = (g3, g1 * g1 * g1 - 4.0 * g3, f1 * f1 * f1 - 4.0 * f3, f3)
    knots = [below + shift for shift in (-1.0, 0.0, 1.0, 2.0)]
    knots = [jnp.where(k < 0.0, k + ANG, jnp.where(k >= ANG, k - ANG, k)) for k in knots]
    return knots, weights


def dense_body(block, group, n_slots, n_prior, refs):
    slot_refs = refs[:n_slots]
    prior = refs[n_slots : n_slots + n_prior]
    out_refs = refs[n_slots + n_prior : len(refs) - bool(group)]
    picks, pieces = [], []
    base = (lax.axis_index("slab") * block).astype(F32)
    tall = 16
    exact = BF16 if block <= 256 else F32
    count = lax.broadcasted_iota(jnp.int32, (tall, 128), 0)
    one, zero = jnp.ones((tall, 128), BF16), jnp.zeros((tall, 128), BF16)

    def spread(rows, j, kind=BF16):
        return jnp.broadcast_to(rows[j : j + 1], (tall, 128)).astype(kind)

    for slot_ref in slot_refs:
        for d in range(slot_ref.shape[0] // 3):
            value = slot_ref[3 * d] * (1.0 / 6.0)
            row = slot_ref[3 * d + 1] - base
            row = jnp.where((row < 0.0) | (row >= block), -1.0, row)
            places, weights = four_weights(slot_ref[3 * d + 2])
            parts = [[p.astype(F32) for p in halves(value * w)] for w in weights]
            for j in range(slot_ref.shape[1]):
                mine = spread(row, j, exact)
                lines = [(count + y).astype(F32).astype(exact) for y in range(0, block, tall)]
                picks.append(jnp.concatenate([jnp.where(l == mine, one, zero) for l in lines], axis=0))
                marks = [spread(p, j) for p in places]
                shares = [[spread(p, j) for p in part] for part in parts]
                columns_of = [[], [], []]
                for y in range(0, ANG, tall):
                    here = (count + y).astype(F32).astype(BF16)
                    hits = [here == mark for mark in marks]
                    for p in range(3):
                        total = zero
                        for hit, share in zip(hits, shares):
                            total = jnp.where(hit, share[p], total)
                        columns_of[p].append(total)
                pieces.append(jnp.concatenate(columns_of[0] + columns_of[1] + columns_of[2], axis=0))
    picks, pieces = jnp.concatenate(picks, axis=1), jnp.concatenate(pieces, axis=1)
    total = lax.dot_general(
        pieces, picks, (((1,), (1,)), ((), ())), preferred_element_type=F32
    )
    total = (total[:ANG] + total[ANG : 2 * ANG] + total[2 * ANG :]).T
    if prior:
        total = total + prior[0][...]
    if group is None:
        out_refs[0][...] = total
    else:
        total_ref = refs[-1]
        rows = block // len(out_refs)
        for i in range(len(out_refs)):
            total_ref[i] = pack(total[i * rows : (i + 1) * rows])
        me = lax.axis_index(group)
        for i, out_ref in enumerate(out_refs):
            out_ref[...] = total_ref[lax.bitwise_xor(me, i)]


def dense(block, group, slots, prior=()):
    members = lax.axis_size(group) if group else 1
    packed = (block // members // 2, 2 * ANG)
    return call(
        lambda *refs: dense_body(block, group, len(slots), len(prior), refs),
        [shape(packed)] * members if group else [shape((block, ANG))],
        (*slots, *prior),
        [VM] * (len(slots) + len(prior)),
        [pltpu.VMEM((members, *packed), F32)] if group else [],
    )


def share_and_add(slots, axis, block, group):
    count = lax.axis_size(axis)
    have = slots
    for k in range(count.bit_length() - 1):
        got = lax.ppermute(have, axis, [(i, i ^ (1 << k)) for i in range(count)])
        if 2 << k < count:
            have = jnp.concatenate([have, got], axis=0)
        else:
            total = dense(block, None, (have,))
            return dense(block, group, (got,), total)


def collect(sums, group):
    count = lax.axis_size(group)
    parts = [sums[0]]
    for i in range(1, count):
        parts.append(lax.ppermute(sums[i], group, [(j, j ^ i) for j in range(count)]))
    return call(add_body, shape((2 * sums[0].shape[0], ANG)), parts, [VM] * count)


def rounds_of(axis):
    return [(axis, first) for first in (0, 1) if swap_pairs(lax.axis_size(axis), first)]


def swap_all(rounds, messages):
    got = []
    for (axis, first), message in zip(rounds, messages):
        got.append(swap(axis, first, message))
    return got


def step_back(
    pressure,
    velocity,
    kappa,
    drive,
    adj_pressure_in,
    adj_velocity_in,
    wall_mask,
    wall_cells,
    wall_rows,
    slot_angle,
    wall_count,
    step,
):
    grid = depth, height, width = pressure.shape
    slots = wall_cells.size
    flat = (1, slots)
    sems = pltpu.SemaphoreType.DMA
    slab_rounds, row_rounds, col_rounds = (rounds_of(a) for a in ("slab", "row", "col"))
    side_rounds = row_rounds + col_rounds
    counts = (len(slab_rounds), len(row_rounds), len(col_rounds))

    outs = call(
        lambda *refs: faces_body(slab_rounds, refs),
        [shape((2, height, width))] * counts[0]
        + [shape(grid)] * 4,
        [stay(x) for x in (pressure, kappa, adj_pressure_in, wall_mask)],
        [HB] * 4,
        [pltpu.VMEM(grid, F32), pltpu.VMEM(grid, jnp.int32), sems((4,))],
    )
    faces, (p_in, q_in, a_in, free) = outs[: counts[0]], outs[counts[0] :]
    slab_got = swap_all(slab_rounds, faces)
    messages = call(
        lambda *refs: sides_body(side_rounds, refs),
        [shape((4, depth, width if axis == "row" else height)) for axis, _ in side_rounds],
        (p_in, q_in, adj_velocity_in, free),
        [VM] * 4,
    )
    side_got = swap_all(side_rounds, messages)
    total, moved, picks, *slot_data = call(
        inner_body,
        [
            shape((3, *grid)),
            shape((3, *grid)),
            shape((depth * height, slots), BF16),
            shape(flat, jnp.int32),
            shape(flat, jnp.int32),
            shape(flat),
            shape(flat, jnp.int32),
        ],
        (
            p_in,
            q_in,
            adj_velocity_in,
            velocity,
            drive,
            *(stay(x.reshape(flat)) for x in (wall_cells, wall_rows, slot_angle)),
            step,
            wall_count.reshape(1),
        ),
        [VM] * 5 + [HB] * 3 + [SM] * 2,
        [sems((3,))],
    )
    lam, mine, *lam_faces = call(
        lambda *refs: main_body(counts, refs),
        [shape((3, *grid)), shape((3, slots // 128, 128))] + [shape((height, width))] * counts[0],
        (
            total,
            moved,
            free,
            picks,
            *slot_data,
            *slab_got,
            *side_got,
        ),
        [VM] * (8 + sum(counts)),
        [pltpu.VMEM((depth * height, width), F32)],
    )
    lam_got = swap_all(slab_rounds, lam_faces)
    part, adj_velocity = call(
        lambda *refs: part_body(counts, refs),
        [shape(grid), shape((3, *grid))],
        (lam, q_in, a_in, *side_got),
        [VM] * (3 + counts[1] + counts[2]),
        [sems((1,))],
        [VM, HB],
    )
    adj_pressure = call(
        lambda *refs: fix_body(refs),
        shape(grid),
        (part, *lam_got),
        [VM] * (1 + counts[0]),
    )
    block = NROWS // lax.axis_size("slab")
    group = ("row", "col")
    total = collect(share_and_add(mine, "slab", block, group), group)
    return (adj_pressure, adj_velocity, total)


def solution(mesh):
    in_specs = (
        P("slab", "row", "col"),
        P(None, "slab", "row", "col"),
        P("slab", "row", "col"),
        P("slab", "row", "col"),
        P("slab", "row", "col"),
        P(None, "slab", "row", "col"),
        P("slab", "row", "col"),
        P("slab", "row", "col", None),
        P("slab", "row", "col", None),
        P("slab", "row", "col", None),
        P("slab", "row", "col"),
        P(),
    )
    out_specs = (
        P("slab", "row", "col"),
        P(None, "slab", "row", "col"),
        P(("slab", "row", "col"), None),
    )
    return jax.shard_map(step_back, mesh=mesh, in_specs=in_specs, out_specs=out_specs, check_vma=False)
```

```python
import jax
import jax.numpy as jnp
from jax import lax
from jax.experimental import pallas as pl
from jax.experimental.pallas import tpu as pltpu
from jax.sharding import PartitionSpec as P


NROWS = 2048
ANG = 64
F32 = jnp.float32
BF16 = jnp.bfloat16
VM = pl.BlockSpec(memory_space=pltpu.VMEM)
SM = pl.BlockSpec(memory_space=pltpu.SMEM)
HB = pl.BlockSpec(memory_space=pltpu.HBM)
LIMIT = pltpu.CompilerParams(vmem_limit_bytes=24 << 20)


def call(body, outs, args, specs, scratch=(), out_specs=None):
    return pl.pallas_call(
        body,
        out_shape=outs,
        in_specs=specs,
        out_specs=jax.tree.map(lambda _: VM, outs) if out_specs is None else out_specs,
        scratch_shapes=list(scratch),
        compiler_params=LIMIT,
        cost_estimate=pl.CostEstimate(flops=1_000_000, bytes_accessed=1_000_000, transcendentals=0),
    )(*args)


def stay(array):
    return pltpu.with_memory_space_constraint(array, pltpu.HBM)


def fetch(pairs, sems):
    copies = [pltpu.make_async_copy(s, d, sems.at[i]) for i, (s, d) in enumerate(pairs)]
    for copy in copies:
        copy.start()
    return copies


def shape(dims, dtype=F32):
    return jax.ShapeDtypeStruct(tuple(dims), dtype)


def is_odd(axis):
    return lax.rem(lax.axis_index(axis), 2) == 1


def swap_pairs(count, first):
    pairs = []
    for low in range(first, count - 1, 2):
        pairs += [(low, low + 1), (low + 1, low)]
    return pairs


def swap(axis, first, message):
    count, lines = lax.axis_size(axis), lax.axis_size("row")
    pairs = swap_pairs(count, first)
    if axis != "slab" or lines % 2:
        return lax.ppermute(message, axis, pairs)
    left = set(range(count)) - {i for i, _ in pairs}
    both = [(i * lines + r, j * lines + r) for i, j in pairs for r in range(lines)]
    both += [(i * lines + r, i * lines + (r ^ 1)) for i in sorted(left) for r in range(lines)]
    return lax.ppermute(message, (axis, "row"), both)


def faces_body(rounds, refs):
    p_ref, k_ref, a_ref, m_ref = refs[:4]
    outs, rest = refs[4 : 4 + len(rounds)], refs[4 + len(rounds) :]
    pv_ref, qv_ref, av_ref, free_ref, kv_ref, mv_ref, sems = rest
    depth = pv_ref.shape[0]
    copies = fetch(((k_ref, kv_ref), (a_ref, av_ref), (p_ref, pv_ref), (m_ref, mv_ref)), sems)
    copies[0].wait()
    copies[1].wait()
    for x in range(depth):
        qv_ref[x] = kv_ref[x] * av_ref[x]
    copies[2].wait()
    odd = is_odd("slab")
    for (_, first), out_ref in zip(rounds, outs):
        at = jnp.where(odd != (first == 1), 0, depth - 1)
        out_ref[0] = pv_ref[at]
        out_ref[1] = qv_ref[at]
    copies[3].wait()
    for x in range(depth):
        free_ref[x] = 1.0 - mv_ref[x].astype(F32)


def sides_body(rounds, refs):
    pv_ref, qv_ref, tv_ref, free_ref, *outs = refs
    depth, height, width = pv_ref.shape
    lanes = lax.broadcasted_iota(jnp.int32, (height, width), 1)
    for (axis, first), out_ref in zip(rounds, outs):
        high = is_odd(axis) == (first == 1)
        sign = jnp.where(high, -0.5, 0.5)
        if axis == "row":
            at = jnp.where(high, height - 1, 0)
            inner = jnp.where(high, height - 2, 1)
            for x in range(depth):
                face, second = pl.ds(at, 1), pl.ds(inner, 1)
                free = free_ref[x, face, :]
                out_ref[0, pl.ds(x, 1), :] = pv_ref[x, face, :]
                out_ref[1, pl.ds(x, 1), :] = qv_ref[x, face, :]
                out_ref[2, pl.ds(x, 1), :] = free * (tv_ref[1, x, face, :] + sign * qv_ref[x, second, :])
                out_ref[3, pl.ds(x, 1), :] = free
        else:
            at = jnp.where(high, width - 1, 0)
            turn = jnp.where(high, 1, width - 1)
            table = jnp.zeros((height, width), F32)
            for x in range(depth):
                free, scaled = free_ref[x], qv_ref[x]
                behind = pltpu.roll(scaled, turn, 1)
                fields = (pv_ref[x], scaled, free * (tv_ref[2, x] + sign * behind), free)
                for f, field in enumerate(fields):
                    lane = f * depth + x
                    moved = pltpu.roll(field, lax.rem(lane - at + width, width), 1)
                    table = jnp.where(lanes == lane, moved, table)
            flipped = table.T
            for f in range(4):
                out_ref[f] = flipped[f * depth : (f + 1) * depth]


def take_halo(axis, refs):
    odd = is_odd(axis)
    first = refs[0][...]
    second = refs[1][...] if len(refs) > 1 else jnp.zeros_like(first)
    me = lax.axis_index(axis)
    low, high = jnp.where(odd, first, second), jnp.where(odd, second, first)
    return jnp.where(me == 0, 0.0, low), jnp.where(me == lax.axis_size(axis) - 1, 0.0, high)


def side(field, axis, low, high):
    size = field.shape[axis]
    at = lax.broadcasted_iota(jnp.int32, field.shape, axis)
    upper = jnp.where(at == size - 1, high, pltpu.roll(field, size - 1, axis))
    lower = jnp.where(at == 0, low, pltpu.roll(field, 1, axis))
    return (upper - lower) * 0.5


def halves(value):
    top = value.astype(BF16)
    rest = value - top.astype(F32)
    mid = rest.astype(BF16)
    return top, mid, (rest - mid.astype(F32)).astype(BF16)


def inner_body(pv_ref, qv_ref, tv_ref, v_ref, d_ref, c_ref, r_ref, g_ref, step_ref, count_ref,
               total_ref, moved_ref, pick_ref, cell_ref, row_ref, angle_ref, live_ref, sems):
    depth, _, width = pv_ref.shape
    copies = fetch(((c_ref, cell_ref), (r_ref, row_ref), (g_ref, angle_ref)), sems)
    slot = lax.broadcasted_iota(jnp.int32, live_ref.shape, 1)
    live_ref[...] = jnp.where(slot < count_ref[0], 1, 0)
    turn = lax.rem(step_ref[0], 97).astype(F32) * 0.5
    phase = jnp.cos(jnp.full((8, width), turn, F32))[:1]
    for x in range(depth):
        p, q = pv_ref[x], qv_ref[x]

        def along(field, ref):
            upper = ref[x + 1] if x + 1 < depth else 0.0
            lower = ref[x - 1] if x > 0 else 0.0
            return (upper - lower) * 0.5, side(field, 0, 0.0, 0.0), side(field, 1, 0.0, 0.0)

        for comp, (slope, gain) in enumerate(zip(along(p, pv_ref), along(q, qv_ref))):
            total_ref[comp, x] = tv_ref[comp, x] + gain
            moved = v_ref[comp, x] - 0.3 * slope
            moved_ref[comp, x] = moved + d_ref[x] * phase if comp == 0 else moved
    for copy in copies:
        copy.wait()
    line = lax.div(cell_ref[...], width)
    at = lax.broadcasted_iota(jnp.int32, pick_ref.shape, 0)
    pick_ref[...] = jnp.where(at == line, 1.0, 0.0).astype(BF16)


def edge_table(low, high, height, width):
    count = low.shape[0]
    lines = []
    for i in range(count):
        lines += [low[i : i + 1], high[i + 1 : i + 2] if i + 1 < count else None]
    lines = [l for l in lines if l is not None]
    fill = jnp.zeros((width - 2 * count, height), F32)
    return jnp.concatenate(lines + [fill, high[:1]], axis=0).T


def main_body(counts, refs):
    total_ref, moved_ref, free_ref, pick_ref, cell_ref, row_ref, angle_ref, live_ref = refs[:8]
    rest = refs[8:]
    n_slab, n_row, n_col = counts
    slab_refs, rest = rest[:n_slab], rest[n_slab:]
    row_refs, rest = rest[:n_row], rest[n_row:]
    col_refs, rest = rest[:n_col], rest[n_col:]
    lam_ref, slot_ref, *face_refs, sens_ref = rest
    _, depth, height, width = total_ref.shape
    slab_low, slab_high = take_halo("slab", slab_refs)
    row_low, row_high = take_halo("row", row_refs)
    col_low, col_high = take_halo("col", col_refs)
    low = jnp.concatenate([col_low[0] * 0.15, col_low[1] * -0.5], axis=0)
    high = jnp.concatenate([col_high[0] * -0.15, col_high[1] * 0.5], axis=0)
    edges = edge_table(low, high, height, width)
    lanes = lax.broadcasted_iota(jnp.int32, (8, width), 1)
    is_edge = (lanes == 0) | (lanes == width - 1)
    tall = lax.broadcasted_iota(jnp.int32, (8, width), 0)
    for x in range(depth):
        for y in range(0, height, 8):
            at = slice(y, y + 8)
            totals = [total_ref[c, x, at] for c in range(3)]
            moves = [moved_ref[c, x, at] for c in range(3)]
            if x == 0:
                totals[0] = totals[0] - 0.5 * slab_low[1, at]
                moves[0] = moves[0] + 0.15 * slab_low[0, at]
            if x == depth - 1:
                totals[0] = totals[0] + 0.5 * slab_high[1, at]
                moves[0] = moves[0] - 0.15 * slab_high[0, at]
            one = slice(x, x + 1)
            if y == 0:
                totals[1] = totals[1] - jnp.where(tall == 0, 0.5 * row_low[1, one], 0.0)
                moves[1] = moves[1] + jnp.where(tall == 0, 0.15 * row_low[0, one], 0.0)
            if y == height - 8:
                totals[1] = totals[1] + jnp.where(tall == 7, 0.5 * row_high[1, one], 0.0)
                moves[1] = moves[1] - jnp.where(tall == 7, 0.15 * row_high[0, one], 0.0)
            for which, terms in ((1, totals), (0, moves)):
                shift = (width - 2 * (which * depth + x)) % width
                turned = pltpu.roll(edges[at], shift, 1) if shift else edges[at]
                terms[2] = terms[2] + jnp.where(is_edge, turned, 0.0)
            free = free_ref[x, at]
            sens = totals[0] * moves[0] + totals[1] * moves[1] + totals[2] * moves[2]
            for c in range(3):
                lam_ref[c, x, at] = free * totals[c]
            sens_ref[pl.ds(x * height + y, 8), :] = -sens
    odd = is_odd("slab")
    for first, face_ref in enumerate(face_refs):
        face_ref[...] = lam_ref[0, jnp.where(odd != (first == 1), 0, depth - 1)]
    cells = cell_ref[...]
    slots = cells.shape[1]
    pieces = jnp.concatenate(halves(sens_ref[...].T), axis=0)
    found = jnp.dot(pieces, pick_ref[...], preferred_element_type=F32)
    found = found[:width] + found[width : 2 * width] + found[2 * width :]
    lane = lax.broadcasted_iota(jnp.int32, (width, slots), 0)
    values = jnp.sum(jnp.where(lane == lax.rem(cells, width), found, 0.0), axis=0, keepdims=True)
    values = jnp.where(live_ref[...] == 1, values, 0.0)
    rows = row_ref[...].astype(F32)
    angles = angle_ref[...]
    for j in range(slots // 128):
        part = slice(128 * j, 128 * (j + 1))
        slot_ref[0, pl.ds(j, 1), :] = values[:, part]
        slot_ref[1, pl.ds(j, 1), :] = rows[:, part]
        slot_ref[2, pl.ds(j, 1), :] = angles[:, part]


def columns(halo, height, width):
    table = jnp.concatenate([halo[2], halo[3]], axis=0)
    table = jnp.concatenate([table, jnp.zeros((width - table.shape[0], height), F32)], axis=0)
    return table.T


def part_body(counts, refs):
    lam_ref, qv_ref, av_ref = refs[:3]
    rest = refs[3:]
    _, n_row, n_col = counts
    row_refs, rest = rest[:n_row], rest[n_row:]
    col_refs, (part_ref, out_ref, sems) = rest[:n_col], rest[n_col:]
    copies = fetch(((lam_ref, out_ref),), sems)
    depth, height, width = av_ref.shape
    row_low, row_high = take_halo("row", row_refs)
    col_low, col_high = (columns(h, height, width) for h in take_halo("col", col_refs))
    for x in range(depth):
        half = 0.5 * qv_ref[x]
        one = slice(x, x + 1)
        free = slice(depth + x, depth + x + 1)
        upper = lam_ref[0, x + 1] if x + 1 < depth else 0.0
        lower = lam_ref[0, x - 1] if x > 0 else 0.0
        row_above = row_high[2, one] - row_high[3, one] * half[height - 1 :]
        row_below = row_low[2, one] + row_low[3, one] * half[:1]
        col_above = col_high[:, one] - col_high[:, free] * half[:, width - 1 :]
        col_below = col_low[:, one] + col_low[:, free] * half[:, :1]
        spread = (
            (upper - lower) * 0.5
            + side(lam_ref[1, x], 0, row_below, row_above)
            + side(lam_ref[2, x], 1, col_below, col_above)
        )
        part_ref[x] = av_ref[x] + 0.3 * spread
    copies[0].wait()


def fix_body(refs):
    part_ref, *face_refs, out_ref = refs
    depth = part_ref.shape[0]
    low, high = take_halo("slab", face_refs)
    for x in range(depth):
        value = part_ref[x]
        if x == 0:
            value = value - 0.15 * low
        if x == depth - 1:
            value = value + 0.15 * high
        out_ref[x] = value


def pack(rows):
    half = rows.shape[0] // 2
    return jnp.concatenate([rows[:half], rows[half:]], axis=1)


def add_body(*refs):
    *parts, out_ref = refs
    total = parts[0][...]
    for part in parts[1:]:
        total = total + part[...]
    out_ref[...] = jnp.concatenate([total[:, :ANG], total[:, ANG:]], axis=0)


def four_weights(angle):
    below = jnp.floor(angle)
    f = angle - below
    g = 1.0 - f
    f3, g3 = f * f * f, g * g * g
    f1, g1 = 1.0 + f, 1.0 + g
    weights = (g3, g1 * g1 * g1 - 4.0 * g3, f1 * f1 * f1 - 4.0 * f3, f3)
    knots = [below + shift for shift in (-1.0, 0.0, 1.0, 2.0)]
    knots = [jnp.where(k < 0.0, k + ANG, jnp.where(k >= ANG, k - ANG, k)) for k in knots]
    return knots, weights


def dense_body(block, group, n_slots, n_prior, refs):
    slot_refs = refs[:n_slots]
    prior = refs[n_slots : n_slots + n_prior]
    out_refs = refs[n_slots + n_prior : len(refs) - bool(group)]
    picks, pieces = [], []
    base = (lax.axis_index("slab") * block).astype(F32)
    tall = 16
    exact = BF16 if block <= 256 else F32
    count = lax.broadcasted_iota(jnp.int32, (tall, 128), 0)
    one, zero = jnp.ones((tall, 128), BF16), jnp.zeros((tall, 128), BF16)

    def spread(rows, j, kind=BF16):
        return jnp.broadcast_to(rows[j : j + 1], (tall, 128)).astype(kind)

    for slot_ref in slot_refs:
        for d in range(slot_ref.shape[0] // 3):
            value = slot_ref[3 * d] * (1.0 / 6.0)
            row = slot_ref[3 * d + 1] - base
            row = jnp.where((row < 0.0) | (row >= block), -1.0, row)
            places, weights = four_weights(slot_ref[3 * d + 2])
            parts = [[p.astype(F32) for p in halves(value * w)] for w in weights]
            for j in range(slot_ref.shape[1]):
                mine = spread(row, j, exact)
                lines = [(count + y).astype(F32).astype(exact) for y in range(0, block, tall)]
                picks.append(jnp.concatenate([jnp.where(l == mine, one, zero) for l in lines], axis=0))
                marks = [spread(p, j) for p in places]
                shares = [[spread(p, j) for p in part] for part in parts]
                columns_of = [[], [], []]
                for y in range(0, ANG, tall):
                    here = (count + y).astype(F32).astype(BF16)
                    hits = [here == mark for mark in marks]
                    for p in range(3):
                        total = zero
                        for hit, share in zip(hits, shares):
                            total = jnp.where(hit, share[p], total)
                        columns_of[p].append(total)
                pieces.append(jnp.concatenate(columns_of[0] + columns_of[1] + columns_of[2], axis=0))
    picks, pieces = jnp.concatenate(picks, axis=1), jnp.concatenate(pieces, axis=1)
    total = lax.dot_general(
        pieces, picks, (((1,), (1,)), ((), ())), preferred_element_type=F32
    )
    total = (total[:ANG] + total[ANG : 2 * ANG] + total[2 * ANG :]).T
    if prior:
        total = total + prior[0][...]
    if group is None:
        out_refs[0][...] = total
    else:
        total_ref = refs[-1]
        rows = block // len(out_refs)
        for i in range(len(out_refs)):
            total_ref[i] = pack(total[i * rows : (i + 1) * rows])
        me = lax.axis_index(group)
        for i, out_ref in enumerate(out_refs):
            out_ref[...] = total_ref[lax.bitwise_xor(me, i)]


def dense(block, group, slots, prior=()):
    members = lax.axis_size(group) if group else 1
    packed = (block // members // 2, 2 * ANG)
    return call(
        lambda *refs: dense_body(block, group, len(slots), len(prior), refs),
        [shape(packed)] * members if group else [shape((block, ANG))],
        (*slots, *prior),
        [VM] * (len(slots) + len(prior)),
        [pltpu.VMEM((members, *packed), F32)] if group else [],
    )


def rounds_of_partners(count):
    bits = count.bit_length() - 1
    return [[d << low for d in range(1, 1 << min(2, bits - low))] for low in range(0, bits, 2)]


def share_and_add(slots, axis, block, group):
    count = lax.axis_size(axis)
    have, got = [slots], []
    for partners in rounds_of_partners(count):
        joined = jnp.concatenate(have + got, axis=0)
        have, got = [joined], []
        for d in partners:
            got.append(lax.ppermute(joined, axis, [(i, i ^ d) for i in range(count)]))
    total = dense(block, None, have)
    return dense(block, group, got, total)


def collect(sums, group):
    count = lax.axis_size(group)
    parts = [sums[0]]
    for i in range(1, count):
        parts.append(lax.ppermute(sums[i], group, [(j, j ^ i) for j in range(count)]))
    return call(add_body, shape((2 * sums[0].shape[0], ANG)), parts, [VM] * count)


def rounds_of(axis):
    return [(axis, first) for first in (0, 1) if swap_pairs(lax.axis_size(axis), first)]


def swap_all(rounds, messages):
    got = []
    for (axis, first), message in zip(rounds, messages):
        got.append(swap(axis, first, message))
    return got


def step_back(
    pressure,
    velocity,
    kappa,
    drive,
    adj_pressure_in,
    adj_velocity_in,
    wall_mask,
    wall_cells,
    wall_rows,
    slot_angle,
    wall_count,
    step,
):
    grid = depth, height, width = pressure.shape
    slots = wall_cells.size
    flat = (1, slots)
    sems = pltpu.SemaphoreType.DMA
    slab_rounds, row_rounds, col_rounds = (rounds_of(a) for a in ("slab", "row", "col"))
    side_rounds = row_rounds + col_rounds
    counts = (len(slab_rounds), len(row_rounds), len(col_rounds))

    outs = call(
        lambda *refs: faces_body(slab_rounds, refs),
        [shape((2, height, width))] * counts[0]
        + [shape(grid)] * 4,
        [stay(x) for x in (pressure, kappa, adj_pressure_in, wall_mask)],
        [HB] * 4,
        [pltpu.VMEM(grid, F32), pltpu.VMEM(grid, jnp.int32), sems((4,))],
    )
    faces, (p_in, q_in, a_in, free) = outs[: counts[0]], outs[counts[0] :]
    slab_got = swap_all(slab_rounds, faces)
    messages = call(
        lambda *refs: sides_body(side_rounds, refs),
        [shape((4, depth, width if axis == "row" else height)) for axis, _ in side_rounds],
        (p_in, q_in, adj_velocity_in, free),
        [VM] * 4,
    )
    side_got = swap_all(side_rounds, messages)
    total, moved, picks, *slot_data = call(
        inner_body,
        [
            shape((3, *grid)),
            shape((3, *grid)),
            shape((depth * height, slots), BF16),
            shape(flat, jnp.int32),
            shape(flat, jnp.int32),
            shape(flat),
            shape(flat, jnp.int32),
        ],
        (
            p_in,
            q_in,
            adj_velocity_in,
            velocity,
            drive,
            *(stay(x.reshape(flat)) for x in (wall_cells, wall_rows, slot_angle)),
            step,
            wall_count.reshape(1),
        ),
        [VM] * 5 + [HB] * 3 + [SM] * 2,
        [sems((3,))],
    )
    lam, mine, *lam_faces = call(
        lambda *refs: main_body(counts, refs),
        [shape((3, *grid)), shape((3, slots // 128, 128))] + [shape((height, width))] * counts[0],
        (
            total,
            moved,
            free,
            picks,
            *slot_data,
            *slab_got,
            *side_got,
        ),
        [VM] * (8 + sum(counts)),
        [pltpu.VMEM((depth * height, width), F32)],
    )
    lam_got = swap_all(slab_rounds, lam_faces)
    part, adj_velocity = call(
        lambda *refs: part_body(counts, refs),
        [shape(grid), shape((3, *grid))],
        (lam, q_in, a_in, *side_got),
        [VM] * (3 + counts[1] + counts[2]),
        [sems((1,))],
        [VM, HB],
    )
    adj_pressure = call(
        lambda *refs: fix_body(refs),
        shape(grid),
        (part, *lam_got),
        [VM] * (1 + counts[0]),
    )
    block = NROWS // lax.axis_size("slab")
    group = ("row", "col")
    total = collect(share_and_add(mine, "slab", block, group), group)
    return (adj_pressure, adj_velocity, total)


def solution(mesh):
    in_specs = (
        P("slab", "row", "col"),
        P(None, "slab", "row", "col"),
        P("slab", "row", "col"),
        P("slab", "row", "col"),
        P("slab", "row", "col"),
        P(None, "slab", "row", "col"),
        P("slab", "row", "col"),
        P("slab", "row", "col", None),
        P("slab", "row", "col", None),
        P("slab", "row", "col", None),
        P("slab", "row", "col"),
        P(),
    )
    out_specs = (
        P("slab", "row", "col"),
        P(None, "slab", "row", "col"),
        P(("slab", "row", "col"), None),
    )
    return jax.shard_map(step_back, mesh=mesh, in_specs=in_specs, out_specs=out_specs, check_vma=False)
```
